32 devices in a mesh: dp: 8 (over y, x, core), fsdp: 4 (over z).
Axes of the slice: x: 2, y: 2, z: 4, core: 2. Of those that a mesh axis runs over, the one named last changes fastest.
Arguments:
- token_ids: int32 [2, 32, 256], P(None, ('dp', 'fsdp')), may hold values from 0 to 51199
- doc_lengths: int32 [2, 32, 3], P(None, ('dp', 'fsdp')), may hold values from 1 to 128, 256 in all within a row
- doc_order: int32 [2, 32, 3], P(None, ('dp', 'fsdp')), may hold values from 0 to 2, each once within a row
- loss_slots: int32 [2, 32, 32], P(None, ('dp', 'fsdp')), may hold values from 0 to 255, as said below
- targets: int32 [2, 32, 32], P(None, ('dp', 'fsdp')), may hold values from 0 to 51199
- loss_mask: int32 [2, 32, 32], P(None, ('dp', 'fsdp')), may hold values from 0 to 1, as said below
- token_table: float32 [51200, 768], P(('dp', 'fsdp'))
- position_table: float32 [256, 768], P(('dp', 'fsdp')), may hold values from -0.21875 to 0.21875
- attend_weight: float32 [2, 768, 2304], P(None, ('dp', 'fsdp')), may hold values from -0.21875 to 0.21875
- project_weight: float32 [2, 768, 768], P(None, ('dp', 'fsdp')), may hold values from -0.875 to 0.875
- expand_weight: float32 [2, 768, 3072], P(None, ('dp', 'fsdp')), may hold values from -0.21875 to 0.21875
- contract_weight: float32 [2, 3072, 768], P(None, ('dp', 'fsdp')), may hold values from -0.109375 to 0.109375
- vector_params: float32 [19968], P(('dp', 'fsdp'))
- table_moments: float32 [2, 51200, 768], P(None, ('dp', 'fsdp'))
- position_moments: float32 [2, 256, 768], P(None, ('dp', 'fsdp'))
- attend_moments: float32 [2, 2, 768, 2304], P(None, None, ('dp', 'fsdp'))
- project_moments: float32 [2, 2, 768, 768], P(None, None, ('dp', 'fsdp'))
- expand_moments: float32 [2, 2, 768, 3072], P(None, None, ('dp', 'fsdp'))
- contract_moments: float32 [2, 2, 3072, 768], P(None, None, ('dp', 'fsdp'))
- vector_moments: float32 [2, 19968], P(None, ('dp', 'fsdp'))
Outputs:
- loss: float32 [], replicated
- grad_norm: float32 [], replicated
- new_table: float32 [51200, 768], P(('dp', 'fsdp'))
- new_positions: float32 [256, 768], P(('dp', 'fsdp'))
- new_attend: float32 [2, 768, 2304], P(None, ('dp', 'fsdp'))
- new_project: float32 [2, 768, 768], P(None, ('dp', 'fsdp'))
- new_expand: float32 [2, 768, 3072], P(None, ('dp', 'fsdp'))
- new_contract: float32 [2, 3072, 768], P(None, ('dp', 'fsdp'))
- new_vectors: float32 [19968], P(('dp', 'fsdp'))
- table_state: float32 [2, 51200, 768], P(None, ('dp', 'fsdp'))
- position_state: float32 [2, 256, 768], P(None, ('dp', 'fsdp'))
- attend_state: float32 [2, 2, 768, 2304], P(None, None, ('dp', 'fsdp'))
- project_state: float32 [2, 2, 768, 768], P(None, None, ('dp', 'fsdp'))
- expand_state: float32 [2, 2, 768, 3072], P(None, None, ('dp', 'fsdp'))
- contract_state: float32 [2, 2, 3072, 768], P(None, None, ('dp', 'fsdp'))
- vector_state: float32 [2, 19968], P(None, ('dp', 'fsdp'))
- table_copy: bfloat16 [51200, 768], P(('dp', 'fsdp'))
- position_copy: bfloat16 [256, 768], P(('dp', 'fsdp'))
- attend_copy: bfloat16 [2, 768, 2304], P(None, ('dp', 'fsdp'))
- project_copy: bfloat16 [2, 768, 768], P(None, ('dp', 'fsdp'))
- expand_copy: bfloat16 [2, 768, 3072], P(None, ('dp', 'fsdp'))
- contract_copy: bfloat16 [2, 3072, 768], P(None, ('dp', 'fsdp'))
- vector_copy: bfloat16 [19968], P(('dp', 'fsdp'))
The draws below stay inside these ranges and needn't reach their ends.
Inputs may be any that keep to these rules, and one draw needn't show every extreme that they name: `doc_lengths`: each row's 3 lengths sum to 256. `doc_order`: each row is a permutation of its 3 places. `loss_slots`: each row's 32 positions are distinct and increasing. `loss_mask`: the first loss position of each row is valid.
All inputs are finite; a program needn't handle non-finite values.
Results may differ from the reference program's by a relative error of at most 0.0095.
Values may be sent and summed in bfloat16 or wider, within the bound.
No kernel may reach another device: no remote copies, remote signals or barrier semaphores. Data moves between devices by JAX's collectives and lax.ppermute only.
A program may use at most 384 MiB of HBM per device.

```python
import math
import jax
import jax.numpy as jnp
import numpy as np
from jax import lax

D = 768
HEADS = 12
HEAD = 64
FF = 3072
VOCAB = 51200
LAYERS = 2
MICRO = 2
SLOT = 256
DOCS = 3
LOSS_ROWS = 32
ROWS = 32
N_FSDP = 4


def draw_loss_slots(key, part):
    row_keys = jax.random.split(key, MICRO * ROWS)

    def one_row(row_key):
        picked = jax.random.permutation(row_key, SLOT)[:LOSS_ROWS]
        return jnp.sort(picked).astype(jnp.int32)
    return jax.vmap(one_row)(row_keys).reshape(MICRO, ROWS, LOSS_ROWS)


def draw_loss_mask(key, part):
    levels = jax.random.randint(key, (MICRO, ROWS, LOSS_ROWS), 0, 4 * ROWS)
    rising = jnp.arange(ROWS, dtype=jnp.int32)[None, :, None]
    counted = (levels < ROWS + 3 * rising).astype(jnp.int32)
    return counted.at[:, :, 0].set(1)


def draw_token_table(key, part):
    rows_each = VOCAB // ROWS
    index = jnp.arange(VOCAB)
    member = index // rows_each % N_FSDP
    fraction = member.astype(jnp.float32) / (N_FSDP - 1)
    scale = (0.8 + 1.2 * fraction) / D ** 0.5
    noise = jnp.clip(jax.random.normal(key, (VOCAB, D), jnp.float32), -6.0, 6.0)
    return noise * scale[:, None]


def draw_vector_params(key, part):
    total = LAYERS * (8 * D + FF) + 2 * D
    block = 8 * D + FF
    index = jnp.arange(total)
    inner = index % block
    final = index >= LAYERS * block
    layer_gain = ((inner < D) | (inner >= 5 * D) & (inner < 6 * D)) & jnp.logical_not(final)
    final_gain = final & (index < LAYERS * block + D)
    noise = jax.random.normal(key, (total,), jnp.float32)
    return jnp.where(layer_gain | final_gain, 1.0 + 0.15 * noise, 0.3 * noise)


def gradient_scale():
    entries = VOCAB * D + SLOT * D + LAYERS * (4 * D * D + 2 * D * FF) + LAYERS * (8 * D + FF) + 2 * D
    return 0.25 / entries ** 0.5


def moment_pair(key, shape, scale):
    first = scale * jax.random.normal(jax.random.fold_in(key, 1), shape, jnp.float32)
    spread = jax.random.uniform(jax.random.fold_in(key, 2), shape, jnp.float32, -1.5, 1.5)
    root = scale * jnp.exp(0.5 * spread)
    return jnp.stack([first, root])


def draw_table_moments(key, part):
    return moment_pair(key, (VOCAB, D), gradient_scale())


def draw_position_moments(key, part):
    return moment_pair(key, (SLOT, D), gradient_scale())


def draw_attend_moments(key, part):
    return moment_pair(key, (LAYERS, D, 3 * D), gradient_scale())


def draw_project_moments(key, part):
    return moment_pair(key, (LAYERS, D, D), gradient_scale())


def draw_expand_moments(key, part):
    return moment_pair(key, (LAYERS, D, FF), gradient_scale())


def draw_contract_moments(key, part):
    return moment_pair(key, (LAYERS, FF, D), gradient_scale())


def draw_vector_moments(key, part):
    return moment_pair(key, (LAYERS * (8 * D + FF) + 2 * D,), 3.0 * gradient_scale())


def place_ends(values, rng, low, largest):
    spot = [jax.random.randint(jax.random.fold_in(rng, axis), (), 0, length) for axis, length in enumerate(values.shape)]
    widest = values.shape.index(max(values.shape))
    neighbour = spot[:widest] + [(spot[widest] + 1) % values.shape[widest]] + spot[widest + 1:]
    return values.at[tuple(spot)].set(low).at[tuple(neighbour)].set(largest)


def block_scale(key, shape, pieces, low, top_value):
    loudness = 1.0
    for axis_at, shards_of in pieces:
        heights = jax.random.uniform(jax.random.fold_in(jax.random.fold_in(key, 6), axis_at), (shards_of,), jnp.float32, low / len(pieces), top_value / len(pieces))
        loudness = loudness * jnp.repeat(jnp.exp(heights), shape[axis_at] // shards_of).reshape((-1,) + (1,) * (len(shape) - 1 - axis_at))
    return loudness


def rank_bounds(amount, lean):
    portions = [(1 << 20) // math.isqrt(rank ** lean) + 1 for rank in range(1, amount + 1)]
    width = 1 + sum(portions) // (1 << 30)
    return np.cumsum(np.array([max(1, weight // width) for weight in portions]))


def ranked(stream_key, extent, number_of, skew):
    table = rank_bounds(number_of, skew)
    pick = jax.random.randint(jax.random.fold_in(stream_key, 1), extent, 0, int(table[number_of - 1]))
    grade = jnp.searchsorted(jnp.asarray(table, jnp.int32), pick, side="right")
    return jax.random.permutation(jax.random.fold_in(stream_key, 2), number_of)[grade].astype(jnp.int32)


def length_profile(count, total, limit, skew):
    portions = [(1 << 20) // math.isqrt(grade ** skew) + 1 for grade in range(2, count + 1)]
    rest, given = total - limit - (count - 1), [1] * (count - 1)
    while rest > 0:
        movable = [i for i in range(count - 1) if given[i] < limit]
        mass, budget = sum([portions[i] for i in movable]), rest
        for i in movable:
            extra = min(limit - given[i], max(1, budget * portions[i] // mass), rest)
            given[i] = given[i] + extra
            rest = rest - extra
    return np.array([limit] + given)


def uneven(rng, number_of, total, reach, slope):
    if number_of == 2:
        one = jax.random.randint(rng, (), max(1, total - reach), min(reach, total - 1) + 1)
        return jnp.stack([one, total - one])
    sizes = jnp.asarray(length_profile(number_of, total, reach, slope), jnp.int32)
    twos = (number_of - 1) // 2
    giver, sink = sizes[1:1 + 2 * twos:2], sizes[2:2 + 2 * twos:2]
    room = jnp.minimum(giver - 1, reach - sink)
    moved = jax.random.randint(jax.random.fold_in(rng, 1), (twos,), 0, 1 << 20) % (room + 1)
    sizes = sizes.at[1:1 + 2 * twos:2].set(giver - moved).at[2:2 + 2 * twos:2].set(sink + moved)
    return sizes[jax.random.permutation(jax.random.fold_in(rng, 2), number_of)]


def bell_draw(own_key, shape, width, most, cuts=(), kind=jnp.bfloat16):
    drawn = width * jax.random.normal(own_key, shape, jnp.float32)
    if cuts:
        drawn = drawn * block_scale(own_key, shape, cuts, -0.22, 0.18)
    return jnp.clip(drawn, -most, most).astype(kind)


def setup_inputs(seed: int = 0) -> dict:
    splits = jax.random.split(jax.random.key(seed), 21)
    token_ids = place_ends(ranked(splits[0], (MICRO, ROWS, SLOT), VOCAB, 2), jax.random.fold_in(splits[0], 3), 0, VOCAB - 1).astype(jnp.int32)
    doc_lengths = jax.vmap(lambda own: uneven(own, DOCS, SLOT, SLOT // 2, 2))(jax.random.split(splits[1], MICRO * ROWS)).reshape((MICRO, ROWS, DOCS)).astype(jnp.int32)
    doc_order = jax.vmap(lambda own: jax.random.permutation(own, DOCS))(jax.random.split(splits[2], MICRO * ROWS)).reshape((MICRO, ROWS, DOCS)).astype(jnp.int32)
    loss_slots = draw_loss_slots(jax.random.fold_in(splits[20], 71), 0)
    targets = place_ends(ranked(splits[4], (MICRO, ROWS, LOSS_ROWS), VOCAB, 2), jax.random.fold_in(splits[4], 3), 0, VOCAB - 1).astype(jnp.int32)
    loss_mask = draw_loss_mask(jax.random.fold_in(splits[20], 71), 0)
    token_table = draw_token_table(jax.random.fold_in(splits[20], 71), 0)
    position_table = bell_draw(splits[7], (SLOT, D), D ** -0.5, 0.21875, ((0, 32),), jnp.float32)
    attend_weight = bell_draw(splits[8], (LAYERS, D, 3 * D), D ** -0.5, 0.21875, ((1, 32),), jnp.float32)
    project_weight = bell_draw(splits[9], (LAYERS, D, D), (D // 16) ** -0.5, 0.875, ((1, 32),), jnp.float32)
    expand_weight = bell_draw(splits[10], (LAYERS, D, FF), D ** -0.5, 0.21875, ((1, 32),), jnp.float32)
    contract_weight = bell_draw(splits[11], (LAYERS, FF, D), FF ** -0.5, 0.109375, ((1, 32),), jnp.float32)
    vector_params = draw_vector_params(jax.random.fold_in(splits[20], 71), 0)
    table_moments = draw_table_moments(jax.random.fold_in(splits[20], 71), 0)
    position_moments = draw_position_moments(jax.random.fold_in(splits[20], 71), 0)
    attend_moments = draw_attend_moments(jax.random.fold_in(splits[20], 71), 0)
    project_moments = draw_project_moments(jax.random.fold_in(splits[20], 71), 0)
    expand_moments = draw_expand_moments(jax.random.fold_in(splits[20], 71), 0)
    contract_moments = draw_contract_moments(jax.random.fold_in(splits[20], 71), 0)
    vector_moments = draw_vector_moments(jax.random.fold_in(splits[20], 71), 0)
    return dict(token_ids=token_ids, doc_lengths=doc_lengths, doc_order=doc_order, loss_slots=loss_slots, targets=targets, loss_mask=loss_mask, token_table=token_table, position_table=position_table, attend_weight=attend_weight, project_weight=project_weight, expand_weight=expand_weight, contract_weight=contract_weight, vector_params=vector_params, table_moments=table_moments, position_moments=position_moments, attend_moments=attend_moments, project_moments=project_moments, expand_moments=expand_moments, contract_moments=contract_moments, vector_moments=vector_moments)


@jax.custom_vjp
def low(v):
    return lax.optimization_barrier(v.astype(jnp.bfloat16)).astype(jnp.float32)

@jax.custom_vjp
def low_back(v):
    return v

def low_keep(v):
    return (low(v), None)

def low_pass(kept, grad):
    return (grad,)

def back_keep(v):
    return (v, None)

def back_low(kept, grad):
    return (low(grad),)
low.defvjp(low_keep, low_pass)
low_back.defvjp(back_keep, back_low)
norm_eps = 1e-05
gelu_scale = 0.7978845608
gelu_cubic = 0.044715
beta_one = 0.5
beta_two = 0.5
learn_rate = 0.03
decay_rate = 0.1
adam_eps = 1e-08
clip_limit = 0.25
adam_step = 3
masked_score = -1e+30
highest = lax.Precision.HIGHEST

def layer_norm(state, gain, bias):
    average = lax.optimization_barrier(jnp.mean(state, axis=-1, keepdims=True))
    centered = state - average
    variance = lax.optimization_barrier(jnp.mean(centered * centered, axis=-1, keepdims=True))
    return centered * lax.rsqrt(variance + norm_eps) * gain + bias

def gelu_tanh(value):
    return 0.5 * value * (1.0 + jnp.tanh(gelu_scale * (value + gelu_cubic * value * value * value)))

def positions_of(lengths, order, slot):
    places = jnp.arange(lengths.shape[0], dtype=jnp.int32)
    place = lax.optimization_barrier(jnp.sum(places[None, :] * (order[None, :] == places[:, None]).astype(jnp.int32), axis=1))
    offset = lax.optimization_barrier(jnp.sum(lengths[None, :] * (place[None, :] < place[:, None]).astype(jnp.int32), axis=1))
    ends = jnp.cumsum(lengths).astype(jnp.int32)
    starts = ends - lengths
    stored = jnp.arange(slot, dtype=jnp.int32)
    document = lax.optimization_barrier(jnp.sum((stored[:, None] >= ends[None, :]).astype(jnp.int32), axis=1))
    onehot = (document[:, None] == places[None, :]).astype(jnp.int32)
    position = stored + lax.optimization_barrier(jnp.sum(onehot * (offset - starts)[None, :], axis=1))
    return (position.astype(jnp.int32), document)

def row_loss(params, row):
    table, position_rows, attend, project, expand, contract, vectors = params
    token_row, lengths, order, slots, target_row, mask_row = row
    position, document = positions_of(lengths, order, SLOT)
    stored = jnp.arange(SLOT, dtype=jnp.int32)
    allowed = (document[:, None] == document[None, :]) & (stored[None, :] <= stored[:, None])
    state = low_back(jnp.take(table, token_row, axis=0)) + jnp.take(position_rows, position, axis=0)
    block = 8 * D + FF
    for layer in range(LAYERS):
        base = layer * block
        gain_one = vectors[base:base + D]
        bias_one = vectors[base + D:base + 2 * D]
        query_bias = vectors[base + 2 * D:base + 3 * D]
        value_bias = vectors[base + 3 * D:base + 4 * D]
        project_bias = vectors[base + 4 * D:base + 5 * D]
        gain_two = vectors[base + 5 * D:base + 6 * D]
        bias_two = vectors[base + 6 * D:base + 7 * D]
        contract_bias = vectors[base + 7 * D:base + 8 * D]
        expand_bias = vectors[base + 8 * D:base + 8 * D + FF]
        normed = low(layer_norm(state, gain_one, bias_one))
        mixed = jnp.dot(normed, attend[layer], precision=highest) + jnp.concatenate([query_bias, jnp.zeros_like(query_bias), value_bias])
        mixed = low(low_back(mixed))
        query = mixed[:, :D].reshape(SLOT, HEADS, HEAD)
        keys = mixed[:, D:2 * D].reshape(SLOT, HEADS, HEAD)
        values = mixed[:, 2 * D:].reshape(SLOT, HEADS, HEAD)
        raw = jnp.einsum('qhd,khd->hqk', query, keys, precision=highest)
        scores = jnp.where(allowed[None], low_back(raw) * HEAD ** (-0.5), masked_score)
        probs = low(jax.nn.softmax(scores, axis=-1))
        attended = jnp.einsum('hqk,khd->qhd', probs, values, precision=highest).reshape(SLOT, D)
        attended = low(low_back(attended))
        state = state + low_back(jnp.dot(attended, project[layer], precision=highest) + project_bias)
        normed_two = low(layer_norm(state, gain_two, bias_two))
        before = low_back(jnp.dot(normed_two, expand[layer], precision=highest) + expand_bias)
        active = low(gelu_tanh(before))
        state = state + low_back(jnp.dot(active, contract[layer], precision=highest) + contract_bias)
    top = LAYERS * block
    final = low(layer_norm(jnp.take(state, slots, axis=0), vectors[top:top + D], vectors[top + D:top + 2 * D]))
    logits = low_back(jnp.dot(final, table.T, precision=highest))
    log_total = jax.nn.logsumexp(logits, axis=-1)
    chosen = jnp.take_along_axis(logits, target_row[:, None], axis=1)[:, 0]
    return jnp.sum(mask_row.astype(jnp.float32) * (log_total - chosen))

def adam_update(weight, moments, grad, decay):
    first = beta_one * moments[0] + (1.0 - beta_one) * grad
    root = jnp.sqrt(beta_two * moments[1] * moments[1] + (1.0 - beta_two) * grad * grad)
    rise = first / (1.0 - beta_one ** adam_step) / (root / (1.0 - beta_two ** adam_step) ** 0.5 + adam_eps)
    fresh = weight - learn_rate * (rise + decay * weight)
    return (fresh, jnp.stack([first, root]), fresh.astype(jnp.bfloat16))

def reference(token_ids, doc_lengths, doc_order, loss_slots, targets, loss_mask, token_table, position_table, attend_weight, project_weight, expand_weight, contract_weight, vector_params, table_moments, position_moments, attend_moments, project_moments, expand_moments, contract_moments, vector_moments):
    weights = (token_table, position_table, attend_weight, project_weight, expand_weight, contract_weight, vector_params)
    rows = tuple((array.reshape((MICRO * ROWS,) + array.shape[2:]) for array in (token_ids, doc_lengths, doc_order, loss_slots, targets, loss_mask)))
    checked = jax.checkpoint(row_loss)

    def total_loss(params):
        lowered = tuple((low(weight) for weight in params))

        def add_row(carry, row):
            return (carry + checked(lowered, row), None)
        total, ignored = lax.scan(add_row, jnp.zeros((), jnp.float32), rows)
        return total
    ce_sum, pullback = jax.vjp(total_loss, weights)
    grads, = pullback(jnp.ones((), jnp.float32))
    count = jnp.sum(loss_mask).astype(jnp.float32)
    scaled = tuple((grad / count for grad in grads))
    grad_norm = jnp.sqrt(sum((jnp.sum(grad * grad) for grad in scaled)))
    factor = clip_limit / jnp.maximum(grad_norm, clip_limit)
    moments = (table_moments, position_moments, attend_moments, project_moments, expand_moments, contract_moments, vector_moments)
    decays = (decay_rate, decay_rate, decay_rate, decay_rate, decay_rate, decay_rate, 0.0)
    table_new, position_new, attend_new, project_new, expand_new, contract_new, vector_new = [adam_update(weight, moment, grad * factor, decay) for weight, moment, grad, decay in zip(weights, moments, scaled, decays)]
    loss = ce_sum / count
    return (loss, grad_norm, table_new[0], position_new[0], attend_new[0], project_new[0], expand_new[0], contract_new[0], vector_new[0], table_new[1], position_new[1], attend_new[1], project_new[1], expand_new[1], contract_new[1], vector_new[1], table_new[2], position_new[2], attend_new[2], project_new[2], expand_new[2], contract_new[2], vector_new[2])
```

```python
import functools

import jax
import jax.numpy as jnp
from jax import lax
from jax.experimental import pallas as pl
from jax.sharding import PartitionSpec as P

HEADS = 12


norm_eps = 1e-05
gelu_scale = 0.7978845608
gelu_cubic = 0.044715
beta_one = 0.5
beta_two = 0.5
learn_rate = 0.03
decay_rate = 0.1
adam_eps = 1e-08
clip_limit = 0.25
adam_step = 3
masked_score = -1e30


def positions_of(lengths, order, slot):
    places = jnp.arange(lengths.shape[0], dtype=jnp.int32)
    place = jnp.sum(places[None, :] * (order[None, :] == places[:, None]).astype(jnp.int32), axis=1)
    offset = jnp.sum(lengths[None, :] * (place[None, :] < place[:, None]).astype(jnp.int32), axis=1)
    ends = jnp.cumsum(lengths)
    starts = ends - lengths
    stored = jnp.arange(slot, dtype=jnp.int32)
    document = jnp.sum((stored[:, None] >= ends[None, :]).astype(jnp.int32), axis=1)
    onehot = (document[:, None] == places[None, :]).astype(jnp.int32)
    position = stored + jnp.sum(onehot * (offset - starts)[None, :], axis=1)
    return (position, document)


def norm_forward(state, gain, bias):
    average = jnp.mean(state, axis=-1, keepdims=True)
    centered = state - average
    inverse = lax.rsqrt(jnp.mean(centered * centered, axis=-1, keepdims=True) + norm_eps)
    scaled = centered * inverse
    return (scaled * gain + bias, scaled, inverse)


def norm_backward(grad, scaled, inverse, gain):
    shaped = grad * gain
    inner = (
        shaped
        - jnp.mean(shaped, axis=-1, keepdims=True)
        - scaled * jnp.mean(shaped * scaled, axis=-1, keepdims=True)
    )
    return (inner * inverse, jnp.sum(grad * scaled, axis=0), jnp.sum(grad, axis=0))


def gelu_tanh(value):
    return 0.5 * value * (1.0 + jnp.tanh(gelu_scale * (value + gelu_cubic * value * value * value)))


def gelu_slope(value):
    bent = jnp.tanh(gelu_scale * (value + gelu_cubic * value * value * value))
    return 0.5 * (1.0 + bent) + 0.5 * value * (1.0 - bent * bent) * gelu_scale * (
        1.0 + 3.0 * gelu_cubic * value * value
    )


def outer_sum(left, right):
    return lax.dot_general(
        left, right, (((0,), (0,)), ((), ())), preferred_element_type=jnp.float32
    )


def times_transpose(left, right):
    return lax.dot_general(
        left, right, (((1,), (1,)), ((), ())), preferred_element_type=jnp.float32
    )


BOTH = ("dp", "fsdp")


def swapped(value, axis, flip):
    size = lax.axis_size(axis)
    return lax.ppermute(value, axis, [(index, index ^ flip) for index in range(size)])


def spread(value):
    count = lax.axis_size("dp") * lax.axis_size("fsdp")
    return lax.all_to_all(jnp.broadcast_to(value[None], (count,) + value.shape), BOTH, 0, 0, tiled=True)


def relative_offsets():
    quads, fsdp = lax.axis_size("dp") // 2, lax.axis_size("fsdp")
    return jnp.array(
        [
            (quad * 2 + core) * fsdp + deep
            for core in range(2)
            for quad in range(quads)
            for deep in range(fsdp)
        ],
        jnp.int32,
    )


def gather_rows(rows):
    quads, fsdp = lax.axis_size("dp") // 2, lax.axis_size("fsdp")
    held = jnp.stack([rows] + [swapped(rows, "fsdp", flip) for flip in range(1, fsdp)])
    held = jnp.stack([held] + [swapped(held, "dp", 2 * flip) for flip in range(1, quads)])
    held = jnp.stack([held, swapped(held, "dp", 1)])
    return held.reshape((-1,) + rows.shape[1:])


def sum_low(pieces):
    total = pieces[0].astype(jnp.float32)
    for piece in pieces[1:]:
        total = total + piece.astype(jnp.float32)
    return total


def scatter_rows(partial):
    quads, fsdp = lax.axis_size("dp") // 2, lax.axis_size("fsdp")
    width = partial.shape[1]
    part = partial.astype(jnp.bfloat16).reshape(2, quads, fsdp, -1, width)
    part = sum_low([part[0], swapped(part[1], "dp", 1)]).astype(jnp.bfloat16)
    part = sum_low(
        [part[0]] + [swapped(part[flip], "dp", 2 * flip) for flip in range(1, quads)]
    ).astype(jnp.bfloat16)
    return sum_low([part[0]] + [swapped(part[flip], "fsdp", flip) for flip in range(1, fsdp)])


def take_one(value, index, axis):
    return lax.dynamic_index_in_dim(value, index, axis, keepdims=False)


def send_core(pieces):
    quads, fsdp = lax.axis_size("dp") // 2, lax.axis_size("fsdp")
    core = lax.axis_index("dp") % 2
    views = [piece.reshape((quads, 2, fsdp) + piece.shape[1:]) for piece in pieces]

    def half(which):
        return jnp.concatenate([take_one(view, which, 1) for view in views], axis=2)

    return [half(core), swapped(half(1 - core), "dp", 1)]


def send_quads(parts):
    quads = lax.axis_size("dp") // 2
    quad = lax.axis_index("dp") // 2
    part = sum_low(parts).astype(jnp.bfloat16)
    return [take_one(part, quad, 0)] + [
        swapped(take_one(part, quad ^ flip, 0), "dp", 2 * flip) for flip in range(1, quads)
    ]


def send_deep(parts):
    fsdp, deep = lax.axis_size("fsdp"), lax.axis_index("fsdp")
    part = sum_low(parts).astype(jnp.bfloat16)
    return [take_one(part, deep, 0)] + [
        swapped(take_one(part, deep ^ flip, 0), "fsdp", flip) for flip in range(1, fsdp)
    ]


def lanes_to_rows(value, devices, width):
    view = value.reshape(devices, -1, value.shape[1])
    return [view[:, :, at : at + width] for at in range(0, value.shape[1], width)]


def rows_to_lanes(value, parts):
    rows = value.shape[0] // parts
    return jnp.concatenate([value[index * rows : (index + 1) * rows] for index in range(parts)], axis=1)


def dotted(left, right, left_at, right_at):
    return lax.dot_general(
        left, right, (((left_at,), (right_at,)), ((), ())), preferred_element_type=jnp.float32
    )


def allowed_of(row_ref, column_ref):
    slot = row_ref.shape[2]
    here = lax.broadcasted_iota(jnp.int32, (slot, slot), 0)
    there = lax.broadcasted_iota(jnp.int32, (slot, slot), 1)
    return (column_ref[0] == row_ref[0]) & (there <= here)


def attend_kernel(head, row_ref, column_ref, mixed_ref, attended_ref, log_ref):
    slot, width = attended_ref.shape
    allowed = allowed_of(row_ref, column_ref)
    for base in range(0, width, 2 * head):
        query, keys, values = [
            mixed_ref[:, part * width + base : part * width + base + 2 * head] for part in range(3)
        ]
        results, logs = [], []
        for at in (0, head):
            raw = dotted(query[:, at : at + head], keys[:, at : at + head], 1, 1)
            scores = jnp.where(allowed, raw * head ** (-0.5), masked_score)
            peak = jnp.max(scores, axis=1, keepdims=True)
            log_total = peak + jnp.log(jnp.sum(jnp.exp(scores - peak), axis=1, keepdims=True))
            probs = jnp.exp(scores - log_total).astype(jnp.bfloat16)
            results.append(dotted(probs, values[:, at : at + head], 1, 0))
            logs.append(jnp.broadcast_to(log_total, (slot, head)))
        attended_ref[:, base : base + 2 * head] = jnp.concatenate(results, axis=1).astype(jnp.bfloat16)
        log_ref[:, base : base + 2 * head] = jnp.concatenate(logs, axis=1)


def attend_back_kernel(head, row_ref, column_ref, mixed_ref, log_ref, grad_ref, out_ref):
    width = grad_ref.shape[1]
    allowed = allowed_of(row_ref, column_ref)
    scale = head ** (-0.5)
    for base in range(0, width, 2 * head):
        query, keys, values = [
            mixed_ref[:, part * width + base : part * width + base + 2 * head] for part in range(3)
        ]
        grads = grad_ref[:, base : base + 2 * head]
        logs = log_ref[:, base : base + 2 * head]
        parts = [[], [], []]
        for at in (0, head):
            q, k, v, g = [value[:, at : at + head] for value in (query, keys, values, grads)]
            scores = jnp.where(allowed, dotted(q, k, 1, 1) * scale, masked_score)
            probs = jnp.exp(scores - logs[:, at : at + 1])
            parts[2].append(dotted(probs.astype(jnp.bfloat16), g, 0, 0))
            slopes = dotted(g, v, 1, 1)
            slopes = probs * (slopes - jnp.sum(probs * slopes, axis=1, keepdims=True))
            slopes = (slopes * scale).astype(jnp.bfloat16)
            parts[0].append(dotted(slopes, k, 1, 0))
            parts[1].append(dotted(slopes, q, 0, 0))
        for which in range(3):
            out_ref[:, which * width + base : which * width + base + 2 * head] = jnp.concatenate(
                parts[which], axis=1
            ).astype(jnp.bfloat16)


def attend_specs(document, width):
    _, slot = document.shape
    return [
        pl.BlockSpec((1, 1, slot), lambda m: (m, 0, 0)),
        pl.BlockSpec((1, slot, 1), lambda m: (m, 0, 0)),
        pl.BlockSpec((slot, 3 * width), lambda m: (m, 0)),
    ], pl.BlockSpec((slot, width), lambda m: (m, 0))


def attend_cost(document, width, dots):
    micro, slot = document.shape
    return pl.CostEstimate(
        flops=2 * dots * micro * slot * slot * width,
        transcendentals=2 * micro * slot * slot * HEADS,
        bytes_accessed=16 * micro * slot * width,
    )


def attend_forward(mixed, document):
    rows, width = mixed.shape[0], mixed.shape[1] // 3
    specs, thin = attend_specs(document, width)
    return pl.pallas_call(
        functools.partial(attend_kernel, width // HEADS),
        grid=(document.shape[0],),
        in_specs=specs,
        out_specs=[thin, thin],
        out_shape=[
            jax.ShapeDtypeStruct((rows, width), jnp.bfloat16),
            jax.ShapeDtypeStruct((rows, width), jnp.float32),
        ],
        cost_estimate=attend_cost(document, width, 2),
        name="attend_forward",
    )(document[:, None, :], document[:, :, None], mixed)


def attend_backward(mixed, document, log_total, grad_attended):
    width = mixed.shape[1] // 3
    specs, thin = attend_specs(document, width)
    return pl.pallas_call(
        functools.partial(attend_back_kernel, width // HEADS),
        grid=(document.shape[0],),
        in_specs=specs + [thin, thin],
        out_specs=specs[2],
        out_shape=jax.ShapeDtypeStruct(mixed.shape, jnp.bfloat16),
        cost_estimate=attend_cost(document, width, 5),
        name="attend_backward",
    )(document[:, None, :], document[:, :, None], mixed, log_total, grad_attended)


def layer_pieces(vectors, base, width, hidden_width):
    pieces = [vectors[base + index * width : base + (index + 1) * width] for index in range(8)]
    return pieces + [vectors[base + 8 * width : base + 8 * width + hidden_width]]


def adam_update(weight, moments, grad, decay):
    first = beta_one * moments[0] + (1.0 - beta_one) * grad
    root = jnp.sqrt(beta_two * moments[1] * moments[1] + (1.0 - beta_two) * grad * grad)
    rise = (
        first / (1.0 - beta_one**adam_step) / (root / (1.0 - beta_two**adam_step) ** 0.5 + adam_eps)
    )
    fresh = weight - learn_rate * (rise + decay * weight)
    return (fresh, jnp.stack([first, root]), fresh.astype(jnp.bfloat16))


def shards(
    token_ids,
    doc_lengths,
    doc_order,
    loss_slots,
    targets,
    loss_mask,
    token_table,
    position_table,
    attend_weight,
    project_weight,
    expand_weight,
    contract_weight,
    vector_params,
    table_moments,
    position_moments,
    attend_moments,
    project_moments,
    expand_moments,
    contract_moments,
    vector_moments,
):
    low = jnp.bfloat16
    fsdp = lax.axis_size("fsdp")
    devices = lax.axis_size("dp") * fsdp
    me = lax.axis_index("dp") * fsdp + lax.axis_index("fsdp")
    micro_count, _, slot = token_ids.shape
    loss_rows = loss_slots.shape[2]
    tokens = micro_count * slot
    width = token_table.shape[1]
    layers, row_share = attend_weight.shape[:2]
    hidden_width = expand_weight.shape[2]
    hidden_share = contract_weight.shape[1]
    rows_each = token_table.shape[0]
    position_share = position_table.shape[0]
    vector_share = vector_params.shape[0]
    block = 8 * width + hidden_width
    vector_rows = -(-vector_share // width)
    small_rows = position_share + vector_rows

    words = token_ids.reshape(tokens)
    owner = words // rows_each
    local = words % rows_each
    earlier = jnp.arange(tokens)[None, :] < jnp.arange(tokens)[:, None]
    first = jnp.logical_not(jnp.any((words[:, None] == words[None, :]) & earlier, axis=1))
    rank = jnp.sum(
        (first[None, :] & (owner[:, None] == owner[None, :]) & (words[None, :] < words[:, None])).astype(jnp.int32),
        axis=1,
    )
    slots_each = max(16, 2 * tokens // devices)
    slots_all = devices * slots_each

    def seats(turn):
        within = rank - turn * slots_each
        return jnp.where((within >= 0) & (within < slots_each), owner * slots_each + within, -1)

    def requests(turn, *marks):
        seat = seats(turn)
        asked = jnp.max(
            jnp.where(seat[None, :] == jnp.arange(slots_all)[:, None], local[None, :], -1), axis=1
        )
        table = jnp.concatenate(
            [asked.reshape(devices, slots_each), jnp.broadcast_to(jnp.max(rank), (devices, 1))]
            + [jnp.broadcast_to(mark.reshape(1, -1), (devices, mark.size)) for mark in marks],
            axis=1,
        )
        return lax.all_to_all(table, BOTH, 0, 0, tiled=True)

    def wanted_of(heard):
        asked = heard[:, :slots_each].reshape(-1)
        return (asked[:, None] == jnp.arange(rows_each)[None, :]).astype(low)

    def seat_matrix(turn):
        return (seats(turn)[:, None] == jnp.arange(slots_all)[None, :]).astype(low)

    table_b = token_table.astype(low)

    def looked_up(turn, heard):
        rows = jnp.dot(wanted_of(heard), table_b, preferred_element_type=jnp.float32).astype(low)
        rows = lax.all_to_all(rows, BOTH, 0, 0, tiled=True)
        return jnp.dot(seat_matrix(turn), rows, preferred_element_type=jnp.float32)

    heard_first = requests(0, targets, loss_mask)
    turns = jnp.max(heard_first[:, slots_each]) // slots_each + 1
    embedded = looked_up(0, heard_first)
    _, embedded = lax.while_loop(
        lambda carry: carry[0] < turns,
        lambda carry: (carry[0] + 1, carry[1] + looked_up(carry[0], requests(carry[0]))),
        (jnp.int32(1), embedded),
    )

    small = jnp.concatenate(
        [
            position_table.astype(low),
            jnp.pad(vector_params.astype(low), (0, vector_rows * width - vector_share)).reshape(vector_rows, width),
        ]
    )
    mixed_share = [
        jnp.concatenate(
            [attend_weight[layer], project_weight[layer], expand_weight[layer]], axis=1
        ).astype(low)
        for layer in range(layers)
    ]
    small_all = spread(small).reshape(devices, small_rows, width)
    mixed_all = [lax.all_gather(share, BOTH, axis=0, tiled=True) for share in mixed_share]
    contract_all = lax.all_gather(contract_weight.astype(low), BOTH, axis=1, tiled=True)
    attend_all = [share[:, : 3 * width] for share in mixed_all]
    project_all = [share[:, 3 * width : 4 * width] for share in mixed_all]
    expand_all = [share[:, 4 * width :] for share in mixed_all]
    position_all = small_all[:, :position_share].reshape(-1, width)
    vectors_f = (
        small_all[:, position_share:].reshape(devices, -1)[:, :vector_share].reshape(-1).astype(jnp.float32)
    )

    order = me ^ relative_offsets()
    marks = jnp.take(heard_first[:, slots_each + 1 :].reshape(devices, 2, -1), order, axis=0)
    target_local = marks[:, 0].reshape(-1) - me * rows_each
    valid = marks[:, 1].reshape(-1).astype(jnp.float32)

    placed = [positions_of(doc_lengths[micro, 0], doc_order[micro, 0], slot) for micro in range(micro_count)]
    position = jnp.concatenate([pair[0] for pair in placed])
    document = jnp.stack([pair[1] for pair in placed])
    stored = jnp.arange(slot, dtype=jnp.int32)
    position_hot = (position[:, None] == stored[None, :]).astype(low)
    state = embedded + jnp.dot(position_hot, position_all, preferred_element_type=jnp.float32)

    saved = []
    for layer in range(layers):
        (
            gain_one,
            bias_one,
            query_bias,
            value_bias,
            project_bias,
            gain_two,
            bias_two,
            contract_bias,
            expand_bias,
        ) = layer_pieces(vectors_f, layer * block, width, hidden_width)
        normed, scaled_one, inverse_one = norm_forward(state, gain_one, bias_one)
        normed_b = normed.astype(low)
        mixed = jnp.dot(
            normed_b, attend_all[layer], preferred_element_type=jnp.float32
        ) + jnp.concatenate([query_bias, jnp.zeros_like(query_bias), value_bias])
        mixed_b = mixed.astype(low)
        attended_b, log_total = attend_forward(mixed_b, document)
        middle = (
            state
            + jnp.dot(attended_b, project_all[layer], preferred_element_type=jnp.float32)
            + project_bias
        )
        normed_two, scaled_two, inverse_two = norm_forward(middle, gain_two, bias_two)
        normed_two_b = normed_two.astype(low)
        before = (
            jnp.dot(normed_two_b, expand_all[layer], preferred_element_type=jnp.float32)
            + expand_bias
        )
        active_b = gelu_tanh(before).astype(low)
        state = (
            middle
            + jnp.dot(active_b, contract_all[layer], preferred_element_type=jnp.float32)
            + contract_bias
        )
        saved.append(
            (
                normed_b,
                scaled_one,
                inverse_one,
                mixed_b,
                log_total,
                attended_b,
                scaled_two,
                inverse_two,
                normed_two_b,
                before,
                active_b,
            )
        )

    top = layers * block
    final_gain = vectors_f[top : top + width]
    final_bias = vectors_f[top + width : top + 2 * width]
    slots = (loss_slots[:, 0] + slot * jnp.arange(micro_count, dtype=jnp.int32)[:, None]).reshape(-1)
    final, scaled_final, inverse_final = norm_forward(
        jnp.take(state, slots, axis=0), final_gain, final_bias
    )
    rows_all = gather_rows(final.astype(low))
    logits = times_transpose(rows_all, table_b)
    hit = jnp.arange(rows_each, dtype=jnp.int32)[None, :] == target_local[:, None]
    peak = jnp.max(logits, axis=1)
    totals = jnp.sum(jnp.exp(logits - peak[:, None]), axis=1)
    chosen = jnp.sum(jnp.where(hit, logits, 0.0), axis=1)
    stats = jnp.stack([peak.reshape(devices, -1), totals.reshape(devices, -1)], axis=1)
    inverse = jnp.argsort(order)
    stats_all = spread(jnp.take(stats, inverse, axis=0).reshape(devices, -1))
    stats_all = stats_all.reshape(devices, devices, 2, -1)
    peak_all = jnp.max(stats_all[:, :, 0], axis=0)
    totals_all = jnp.sum(stats_all[:, :, 1] * jnp.exp(stats_all[:, :, 0] - peak_all[None]), axis=0)
    log_rows = jnp.take(peak_all + jnp.log(totals_all), order, axis=0).reshape(-1)
    own = micro_count * loss_rows
    entropy_local = jnp.sum(log_rows[:own] * valid[:own]) - jnp.sum(chosen * valid)
    grad_logits = (
        (jnp.exp(logits - log_rows[:, None]) - hit.astype(jnp.float32)) * valid[:, None]
    ).astype(low)
    grad_final = scatter_rows(jnp.dot(grad_logits, table_b, preferred_element_type=jnp.float32))
    table_grad = outer_sum(grad_logits, rows_all)
    grad_rows, grad_final_gain, grad_final_bias = norm_backward(
        grad_final, scaled_final, inverse_final, final_gain
    )
    slot_hot = (jnp.arange(tokens, dtype=jnp.int32)[:, None] == slots[None, :]).astype(jnp.float32)
    grad_state = jnp.dot(slot_hot, grad_rows, precision=lax.Precision.HIGHEST)

    layer_grads = [None] * layers
    wide_sent, narrow_sent = [None] * layers, [None] * layers
    for layer in reversed(range(layers)):
        (
            normed_b,
            scaled_one,
            inverse_one,
            mixed_b,
            log_total,
            attended_b,
            scaled_two,
            inverse_two,
            normed_two_b,
            before,
            active_b,
        ) = saved[layer]
        gain_one, _, _, _, _, gain_two, _, _, _ = layer_pieces(vectors_f, layer * block, width, hidden_width)
        grad_out = grad_state.astype(low)
        contract_grad = outer_sum(active_b, grad_out).astype(low)
        grad_contract_bias = jnp.sum(grad_out.astype(jnp.float32), axis=0)
        grad_active = times_transpose(grad_out, contract_all[layer])
        grad_before = (grad_active * gelu_slope(before)).astype(low)
        expand_grad = outer_sum(normed_two_b, grad_before).astype(low)
        wide_sent[layer] = send_core(
            [contract_grad.reshape(devices, hidden_share, width)]
            + lanes_to_rows(expand_grad, devices, width)
        )
        grad_expand_bias = jnp.sum(grad_before.astype(jnp.float32), axis=0)
        grad_normed_two = times_transpose(grad_before, expand_all[layer])
        grad_mid, grad_gain_two, grad_bias_two = norm_backward(
            grad_normed_two, scaled_two, inverse_two, gain_two
        )
        grad_middle = grad_state + grad_mid
        grad_project = grad_middle.astype(low)
        wide_sent[layer] = send_quads(wide_sent[layer])
        project_grad = outer_sum(attended_b, grad_project).astype(low)
        grad_project_bias = jnp.sum(grad_project.astype(jnp.float32), axis=0)
        grad_attended = times_transpose(grad_project, project_all[layer]).astype(low)
        if layer < layers - 1:
            wide_sent[layer + 1] = send_deep(wide_sent[layer + 1])
        grad_mixed = attend_backward(mixed_b, document, log_total, grad_attended)
        attend_grad = outer_sum(normed_b, grad_mixed).astype(low)
        narrow_sent[layer] = send_core(
            lanes_to_rows(attend_grad, devices, width) + lanes_to_rows(project_grad, devices, width)
        )
        grad_mixed_f = grad_mixed.astype(jnp.float32)
        grad_query_bias = jnp.sum(grad_mixed_f[:, :width], axis=0)
        grad_value_bias = jnp.sum(grad_mixed_f[:, 2 * width :], axis=0)
        grad_normed = times_transpose(grad_mixed, attend_all[layer])
        grad_in, grad_gain_one, grad_bias_one = norm_backward(
            grad_normed, scaled_one, inverse_one, gain_one
        )
        grad_state = grad_middle + grad_in
        narrow_sent[layer] = send_quads(narrow_sent[layer])
        layer_grads[layer] = jnp.concatenate(
            [
                grad_gain_one,
                grad_bias_one,
                grad_query_bias,
                grad_value_bias,
                grad_project_bias,
                grad_gain_two,
                grad_bias_two,
                grad_contract_bias,
                grad_expand_bias,
            ]
        )

    grad_embedded = grad_state.astype(low)
    position_grad = outer_sum(position_hot, grad_embedded).astype(low)
    vector_grad = jnp.concatenate(layer_grads + [grad_final_gain, grad_final_bias])
    vector_grad = jnp.pad(
        vector_grad.astype(low).reshape(devices, vector_share),
        ((0, 0), (0, vector_rows * width - vector_share)),
    )

    def returned(turn):
        return outer_sum(seat_matrix(turn), grad_embedded).astype(low).reshape(devices, slots_each, width)

    came = lax.all_to_all(
        jnp.concatenate(
            [
                returned(0),
                position_grad.reshape(devices, position_share, width),
                vector_grad.reshape(devices, vector_rows, width),
            ],
            axis=1,
        ),
        BOTH,
        0,
        0,
        tiled=True,
    )
    small_sum = jnp.sum(came[:, slots_each:].astype(jnp.float32), axis=0)
    table_grad = table_grad + outer_sum(wanted_of(heard_first), came[:, :slots_each].reshape(slots_all, width))

    def later_turn(carry):
        turn, total = carry
        rows = lax.all_to_all(returned(turn), BOTH, 0, 0, tiled=True).reshape(slots_all, width)
        return (turn + 1, total + outer_sum(wanted_of(requests(turn)), rows))

    _, table_sum = lax.while_loop(lambda carry: carry[0] < turns, later_turn, (jnp.int32(1), table_grad))
    for layer in range(1, layers):
        narrow_sent[layer] = send_deep(narrow_sent[layer])
    wide_sent[0] = send_deep(wide_sent[0])
    narrow_sent[0] = send_deep(narrow_sent[0])
    wide_sums = [sum_low(sent) for sent in wide_sent]
    narrow_sums = [sum_low(sent) for sent in narrow_sent]

    contract_sum = jnp.stack([total[:hidden_share] for total in wide_sums])
    expand_sum = jnp.stack(
        [rows_to_lanes(total[hidden_share:], hidden_width // width) for total in wide_sums]
    )
    attend_sum = jnp.stack([rows_to_lanes(total[: 3 * row_share], 3) for total in narrow_sums])
    project_sum = jnp.stack([total[3 * row_share : 4 * row_share] for total in narrow_sums])
    position_sum = small_sum[:position_share]
    vector_sum = small_sum[position_share:].reshape(-1)[:vector_share]

    sums = (table_sum, position_sum, attend_sum, project_sum, expand_sum, contract_sum, vector_sum)
    squares = jnp.zeros((), jnp.float32)
    for grad in sums:
        squares = squares + jnp.sum(grad * grad)
    scalars = jnp.stack([squares, entropy_local, jnp.sum(loss_mask).astype(jnp.float32)])
    square_total, entropy_total, count = jnp.sum(spread(scalars).reshape(devices, 3), axis=0)
    grad_norm = jnp.sqrt(square_total) / count
    factor = clip_limit / jnp.maximum(grad_norm, clip_limit)
    loss = entropy_total / count
    weights = (
        token_table,
        position_table,
        attend_weight,
        project_weight,
        expand_weight,
        contract_weight,
        vector_params,
    )
    moments = (
        table_moments,
        position_moments,
        attend_moments,
        project_moments,
        expand_moments,
        contract_moments,
        vector_moments,
    )
    decays = (decay_rate, decay_rate, decay_rate, decay_rate, decay_rate, decay_rate, 0.0)
    table_new, position_new, attend_new, project_new, expand_new, contract_new, vector_new = [
        adam_update(weight, moment, grad / count * factor, decay)
        for weight, moment, grad, decay in zip(weights, moments, sums, decays)
    ]
    return (
        loss,
        grad_norm,
        table_new[0],
        position_new[0],
        attend_new[0],
        project_new[0],
        expand_new[0],
        contract_new[0],
        vector_new[0],
        table_new[1],
        position_new[1],
        attend_new[1],
        project_new[1],
        expand_new[1],
        contract_new[1],
        vector_new[1],
        table_new[2],
        position_new[2],
        attend_new[2],
        project_new[2],
        expand_new[2],
        contract_new[2],
        vector_new[2],
    )


def solution(mesh):
    return jax.shard_map(
        shards,
        mesh=mesh,
        in_specs=(
            P(None, ("dp", "fsdp"), None),
            P(None, ("dp", "fsdp"), None),
            P(None, ("dp", "fsdp"), None),
            P(None, ("dp", "fsdp"), None),
            P(None, ("dp", "fsdp"), None),
            P(None, ("dp", "fsdp"), None),
            P(("dp", "fsdp"), None),
            P(("dp", "fsdp"), None),
            P(None, ("dp", "fsdp"), None),
            P(None, ("dp", "fsdp"), None),
            P(None, ("dp", "fsdp"), None),
            P(None, ("dp", "fsdp"), None),
            P(("dp", "fsdp")),
            P(None, ("dp", "fsdp"), None),
            P(None, ("dp", "fsdp"), None),
            P(None, None, ("dp", "fsdp"), None),
            P(None, None, ("dp", "fsdp"), None),
            P(None, None, ("dp", "fsdp"), None),
            P(None, None, ("dp", "fsdp"), None),
            P(None, ("dp", "fsdp")),
        ),
        out_specs=(
            P(),
            P(),
            P(("dp", "fsdp"), None),
            P(("dp", "fsdp"), None),
            P(None, ("dp", "fsdp"), None),
            P(None, ("dp", "fsdp"), None),
            P(None, ("dp", "fsdp"), None),
            P(None, ("dp", "fsdp"), None),
            P(("dp", "fsdp")),
            P(None, ("dp", "fsdp"), None),
            P(None, ("dp", "fsdp"), None),
            P(None, None, ("dp", "fsdp"), None),
            P(None, None, ("dp", "fsdp"), None),
            P(None, None, ("dp", "fsdp"), None),
            P(None, None, ("dp", "fsdp"), None),
            P(None, ("dp", "fsdp")),
            P(("dp", "fsdp"), None),
            P(("dp", "fsdp"), None),
            P(None, ("dp", "fsdp"), None),
            P(None, ("dp", "fsdp"), None),
            P(None, ("dp", "fsdp"), None),
            P(None, ("dp", "fsdp"), None),
            P(("dp", "fsdp")),
        ),
        check_vma=False,
    )
```

```python
import functools

import jax
import jax.numpy as jnp
from jax import lax
from jax.experimental import pallas as pl
from jax.experimental.pallas import tpu as pltpu
from jax.sharding import PartitionSpec as P

HEADS = 12


norm_eps = 1e-05
gelu_scale = 0.7978845608
gelu_cubic = 0.044715
beta_one = 0.5
beta_two = 0.5
learn_rate = 0.03
decay_rate = 0.1
adam_eps = 1e-08
clip_limit = 0.25
adam_step = 3
masked_score = -1e30


def positions_of(lengths, order, slot):
    places = jnp.arange(lengths.shape[0], dtype=jnp.int32)
    place = jnp.sum(places[None, :] * (order[None, :] == places[:, None]).astype(jnp.int32), axis=1)
    offset = jnp.sum(lengths[None, :] * (place[None, :] < place[:, None]).astype(jnp.int32), axis=1)
    ends = jnp.cumsum(lengths)
    starts = ends - lengths
    stored = jnp.arange(slot, dtype=jnp.int32)
    document = jnp.sum((stored[:, None] >= ends[None, :]).astype(jnp.int32), axis=1)
    onehot = (document[:, None] == places[None, :]).astype(jnp.int32)
    position = stored + jnp.sum(onehot * (offset - starts)[None, :], axis=1)
    return (position, document)


def norm_forward(state, gain, bias):
    average = jnp.mean(state, axis=-1, keepdims=True)
    centered = state - average
    inverse = lax.rsqrt(jnp.mean(centered * centered, axis=-1, keepdims=True) + norm_eps)
    scaled = centered * inverse
    return (scaled * gain + bias, scaled, inverse)


def norm_backward(grad, scaled, inverse, gain):
    shaped = grad * gain
    inner = (
        shaped
        - jnp.mean(shaped, axis=-1, keepdims=True)
        - scaled * jnp.mean(shaped * scaled, axis=-1, keepdims=True)
    )
    return (inner * inverse, jnp.sum(grad * scaled, axis=0), jnp.sum(grad, axis=0))


def gelu_tanh(value):
    return 0.5 * value * (1.0 + jnp.tanh(gelu_scale * (value + gelu_cubic * value * value * value)))


def gelu_slope(value):
    bent = jnp.tanh(gelu_scale * (value + gelu_cubic * value * value * value))
    return 0.5 * (1.0 + bent) + 0.5 * value * (1.0 - bent * bent) * gelu_scale * (
        1.0 + 3.0 * gelu_cubic * value * value
    )


def outer_sum(left, right):
    return lax.dot_general(
        left, right, (((0,), (0,)), ((), ())), preferred_element_type=jnp.float32
    )


def times_transpose(left, right):
    return lax.dot_general(
        left, right, (((1,), (1,)), ((), ())), preferred_element_type=jnp.float32
    )


BOTH = ("dp", "fsdp")


def swapped(value, axis, flip):
    size = lax.axis_size(axis)
    return lax.ppermute(value, axis, [(index, index ^ flip) for index in range(size)])


def spread(value):
    count = lax.axis_size("dp") * lax.axis_size("fsdp")
    return lax.all_to_all(jnp.broadcast_to(value[None], (count,) + value.shape), BOTH, 0, 0, tiled=True)


def relative_offsets():
    quads, fsdp = lax.axis_size("dp") // 2, lax.axis_size("fsdp")
    return jnp.array(
        [
            (quad * 2 + core) * fsdp + deep
            for core in range(2)
            for quad in range(quads)
            for deep in range(fsdp)
        ],
        jnp.int32,
    )


def gather_rows(rows):
    quads, fsdp = lax.axis_size("dp") // 2, lax.axis_size("fsdp")
    held = jnp.stack([rows] + [swapped(rows, "fsdp", flip) for flip in range(1, fsdp)])
    held = jnp.stack([held] + [swapped(held, "dp", 2 * flip) for flip in range(1, quads)])
    held = jnp.stack([held, swapped(held, "dp", 1)])
    return held.reshape((-1,) + rows.shape[1:])


def sum_low(pieces):
    total = pieces[0].astype(jnp.float32)
    for piece in pieces[1:]:
        total = total + piece.astype(jnp.float32)
    return total


def head_quads(value, flip):
    return swapped(value, "dp", 2 * flip)


def scatter_rows(partial):
    quads, fsdp = lax.axis_size("dp") // 2, lax.axis_size("fsdp")
    width = partial.shape[1]
    part = partial.astype(jnp.bfloat16).reshape(2, quads, fsdp, -1, width)
    part = sum_low([part[0], swapped(part[1], "dp", 1)]).astype(jnp.bfloat16)
    part = sum_low(
        [part[0]] + [head_quads(part[flip], flip) for flip in range(1, quads)]
    ).astype(jnp.bfloat16)
    return sum_low([part[0]] + [swapped(part[flip], "fsdp", flip) for flip in range(1, fsdp)])


def take_one(value, index, axis):
    return lax.dynamic_index_in_dim(value, index, axis, keepdims=False)


def send_core(pieces):
    quads, fsdp = lax.axis_size("dp") // 2, lax.axis_size("fsdp")
    core = lax.axis_index("dp") % 2
    views = [piece.reshape((quads, 2, fsdp) + piece.shape[1:]) for piece in pieces]

    def half(which):
        return jnp.concatenate([take_one(view, which, 1) for view in views], axis=2)

    return [half(core), swapped(half(1 - core), "dp", 1)]


def send_quads(parts):
    quads = lax.axis_size("dp") // 2
    quad = lax.axis_index("dp") // 2
    part = sum_low(parts).astype(jnp.bfloat16)
    return [take_one(part, quad, 0)] + [
        swapped(take_one(part, quad ^ flip, 0), "dp", 2 * flip) for flip in range(1, quads)
    ]


def send_deep(parts):
    fsdp, deep = lax.axis_size("fsdp"), lax.axis_index("fsdp")
    part = sum_low(parts).astype(jnp.bfloat16)
    return [take_one(part, deep, 0)] + [
        swapped(take_one(part, deep ^ flip, 0), "fsdp", flip) for flip in range(1, fsdp)
    ]


def lanes_to_rows(value, devices, width):
    view = value.reshape(devices, -1, value.shape[1])
    return [view[:, :, at : at + width] for at in range(0, value.shape[1], width)]


def rows_to_lanes(value, parts):
    rows = value.shape[0] // parts
    return jnp.concatenate([value[index * rows : (index + 1) * rows] for index in range(parts)], axis=1)


def dotted(left, right, left_at, right_at):
    return lax.dot_general(
        left, right, (((left_at,), (right_at,)), ((), ())), preferred_element_type=jnp.float32
    )


def allowed_of(row_ref, column_ref):
    slot = row_ref.shape[2]
    here = lax.broadcasted_iota(jnp.int32, (slot, slot), 0)
    there = lax.broadcasted_iota(jnp.int32, (slot, slot), 1)
    return (column_ref[0] == row_ref[0]) & (there <= here)


def attend_kernel(head, row_ref, column_ref, mixed_ref, attended_ref, log_ref):
    slot, width = attended_ref.shape
    allowed = allowed_of(row_ref, column_ref)
    for base in range(0, width, 2 * head):
        query, keys, values = [
            mixed_ref[:, part * width + base : part * width + base + 2 * head] for part in range(3)
        ]
        results, logs = [], []
        for at in (0, head):
            raw = dotted(query[:, at : at + head], keys[:, at : at + head], 1, 1)
            scores = jnp.where(allowed, raw * head ** (-0.5), masked_score)
            peak = jnp.max(scores, axis=1, keepdims=True)
            log_total = peak + jnp.log(jnp.sum(jnp.exp(scores - peak), axis=1, keepdims=True))
            probs = jnp.exp(scores - log_total).astype(jnp.bfloat16)
            results.append(dotted(probs, values[:, at : at + head], 1, 0))
            logs.append(jnp.broadcast_to(log_total, (slot, head)))
        attended_ref[:, base : base + 2 * head] = jnp.concatenate(results, axis=1).astype(jnp.bfloat16)
        log_ref[:, base : base + 2 * head] = jnp.concatenate(logs, axis=1)


def attend_back_kernel(head, row_ref, column_ref, mixed_ref, log_ref, grad_ref, out_ref):
    width = grad_ref.shape[1]
    allowed = allowed_of(row_ref, column_ref)
    scale = head ** (-0.5)
    for base in range(0, width, 2 * head):
        query, keys, values = [
            mixed_ref[:, part * width + base : part * width + base + 2 * head] for part in range(3)
        ]
        grads = grad_ref[:, base : base + 2 * head]
        logs = log_ref[:, base : base + 2 * head]
        parts = [[], [], []]
        for at in (0, head):
            q, k, v, g = [value[:, at : at + head] for value in (query, keys, values, grads)]
            scores = jnp.where(allowed, dotted(q, k, 1, 1) * scale, masked_score)
            probs = jnp.exp(scores - logs[:, at : at + 1])
            parts[2].append(dotted(probs.astype(jnp.bfloat16), g, 0, 0))
            slopes = dotted(g, v, 1, 1)
            slopes = probs * (slopes - jnp.sum(probs * slopes, axis=1, keepdims=True))
            slopes = (slopes * scale).astype(jnp.bfloat16)
            parts[0].append(dotted(slopes, k, 1, 0))
            parts[1].append(dotted(slopes, q, 0, 0))
        for which in range(3):
            out_ref[:, which * width + base : which * width + base + 2 * head] = jnp.concatenate(
                parts[which], axis=1
            ).astype(jnp.bfloat16)


def attend_specs(document, width):
    _, slot = document.shape
    return [
        pl.BlockSpec((1, 1, slot), lambda m: (m, 0, 0)),
        pl.BlockSpec((1, slot, 1), lambda m: (m, 0, 0)),
        pl.BlockSpec((slot, 3 * width), lambda m: (m, 0)),
    ], pl.BlockSpec((slot, width), lambda m: (m, 0))


def attend_cost(document, width, dots):
    micro, slot = document.shape
    return pl.CostEstimate(
        flops=2 * dots * micro * slot * slot * width,
        transcendentals=2 * micro * slot * slot * HEADS,
        bytes_accessed=16 * micro * slot * width,
    )


def attend_forward(mixed, document):
    rows, width = mixed.shape[0], mixed.shape[1] // 3
    specs, thin = attend_specs(document, width)
    return pl.pallas_call(
        functools.partial(attend_kernel, width // HEADS),
        grid=(document.shape[0],),
        in_specs=specs,
        out_specs=[thin, thin],
        out_shape=[
            jax.ShapeDtypeStruct((rows, width), jnp.bfloat16),
            jax.ShapeDtypeStruct((rows, width), jnp.float32),
        ],
        cost_estimate=attend_cost(document, width, 2),
        name="attend_forward",
    )(document[:, None, :], document[:, :, None], mixed)


def attend_backward(mixed, document, log_total, grad_attended):
    width = mixed.shape[1] // 3
    specs, thin = attend_specs(document, width)
    return pl.pallas_call(
        functools.partial(attend_back_kernel, width // HEADS),
        grid=(document.shape[0],),
        in_specs=specs + [thin, thin],
        out_specs=specs[2],
        out_shape=jax.ShapeDtypeStruct(mixed.shape, jnp.bfloat16),
        cost_estimate=attend_cost(document, width, 5),
        name="attend_backward",
    )(document[:, None, :], document[:, :, None], mixed, log_total, grad_attended)


def layer_pieces(vectors, base, width, hidden_width):
    pieces = [vectors[base + index * width : base + (index + 1) * width] for index in range(8)]
    return pieces + [vectors[base + 8 * width : base + 8 * width + hidden_width]]


def adam_update(weight, moments, grad, decay):
    first = beta_one * moments[0] + (1.0 - beta_one) * grad
    root = jnp.sqrt(beta_two * moments[1] * moments[1] + (1.0 - beta_two) * grad * grad)
    rise = (
        first / (1.0 - beta_one**adam_step) / (root / (1.0 - beta_two**adam_step) ** 0.5 + adam_eps)
    )
    fresh = weight - learn_rate * (rise + decay * weight)
    return (fresh, jnp.stack([first, root]), fresh.astype(jnp.bfloat16))


def adam_kernel(decay, scale_ref, weight_ref, moments_ref, grad_ref, fresh_ref, state_ref, copy_ref):
    fresh, state, copy = adam_update(
        weight_ref[...], moments_ref[...], grad_ref[...] / scale_ref[0] * scale_ref[1], decay
    )
    fresh_ref[...], state_ref[...], copy_ref[...] = fresh, state, copy


def adam_blocks(weight, moments, grad, count, factor, decay):
    rows, width = weight.shape
    step = rows if rows <= 320 else max(size for size in range(16, 321, 16) if rows % size == 0)
    flat = pl.BlockSpec((step, width), lambda at: (at, 0))
    pair = pl.BlockSpec((2, step, width), lambda at: (0, at, 0))
    return pl.pallas_call(
        functools.partial(adam_kernel, decay),
        grid=(rows // step,),
        in_specs=[pl.BlockSpec(memory_space=pltpu.SMEM), flat, pair, flat],
        out_specs=[flat, pair, flat],
        out_shape=[
            jax.ShapeDtypeStruct(weight.shape, jnp.float32),
            jax.ShapeDtypeStruct(moments.shape, jnp.float32),
            jax.ShapeDtypeStruct(weight.shape, jnp.bfloat16),
        ],
        cost_estimate=pl.CostEstimate(
            flops=20 * rows * width, transcendentals=rows * width, bytes_accessed=30 * rows * width
        ),
        name="adam_blocks",
    )(jnp.stack([count, factor]), weight, moments, grad)


def shards(
    token_ids,
    doc_lengths,
    doc_order,
    loss_slots,
    targets,
    loss_mask,
    token_table,
    position_table,
    attend_weight,
    project_weight,
    expand_weight,
    contract_weight,
    vector_params,
    table_moments,
    position_moments,
    attend_moments,
    project_moments,
    expand_moments,
    contract_moments,
    vector_moments,
):
    low = jnp.bfloat16
    fsdp = lax.axis_size("fsdp")
    devices = lax.axis_size("dp") * fsdp
    me = lax.axis_index("dp") * fsdp + lax.axis_index("fsdp")
    micro_count, _, slot = token_ids.shape
    loss_rows = loss_slots.shape[2]
    tokens = micro_count * slot
    width = token_table.shape[1]
    layers, row_share = attend_weight.shape[:2]
    hidden_width = expand_weight.shape[2]
    hidden_share = contract_weight.shape[1]
    rows_each = token_table.shape[0]
    position_share = position_table.shape[0]
    vector_share = vector_params.shape[0]
    block = 8 * width + hidden_width
    vector_rows = -(-vector_share // width)
    small_rows = -(-(position_share + vector_rows) // 16) * 16

    words = token_ids.reshape(tokens)
    owner = words // rows_each
    local = words % rows_each
    earlier = jnp.arange(tokens)[None, :] < jnp.arange(tokens)[:, None]
    first = jnp.logical_not(jnp.any((words[:, None] == words[None, :]) & earlier, axis=1))
    rank = jnp.sum(
        (first[None, :] & (owner[:, None] == owner[None, :]) & (words[None, :] < words[:, None])).astype(jnp.int32),
        axis=1,
    )
    slots_each = max(16, 2 * tokens // devices)
    slots_all = devices * slots_each

    def seats(turn):
        within = rank - turn * slots_each
        return jnp.where((within >= 0) & (within < slots_each), owner * slots_each + within, -1)

    def requests(turn, *marks):
        seat = seats(turn)
        asked = jnp.max(
            jnp.where(seat[None, :] == jnp.arange(slots_all)[:, None], local[None, :], -1), axis=1
        )
        table = jnp.concatenate(
            [asked.reshape(devices, slots_each), jnp.broadcast_to(jnp.max(rank), (devices, 1))]
            + [jnp.broadcast_to(mark.reshape(1, -1), (devices, mark.size)) for mark in marks],
            axis=1,
        )
        return lax.all_to_all(table, BOTH, 0, 0, tiled=True)

    def wanted_of(heard):
        asked = heard[:, :slots_each].reshape(-1)
        return (asked[:, None] == jnp.arange(rows_each)[None, :]).astype(low)

    def seat_matrix(turn):
        return (seats(turn)[:, None] == jnp.arange(slots_all)[None, :]).astype(low)

    table_b = token_table.astype(low)

    def looked_up(turn, heard):
        rows = jnp.dot(wanted_of(heard), table_b, preferred_element_type=jnp.float32).astype(low)
        rows = lax.all_to_all(rows, BOTH, 0, 0, tiled=True)
        return jnp.dot(seat_matrix(turn), rows, preferred_element_type=jnp.float32)

    heard_first = requests(0, targets, loss_mask)
    fold = hidden_share // row_share
    position_lanes = position_share * width // row_share
    vector_lanes = 128 * -(-vector_share // (128 * row_share))
    small = [
        position_table.astype(low).reshape(row_share, position_lanes),
        jnp.pad(vector_params.astype(low), (0, row_share * vector_lanes - vector_share)).reshape(
            row_share, vector_lanes
        ),
    ]
    mixed_share = [
        jnp.concatenate(
            (small if layer == 0 else [])
            + [attend_weight[layer].astype(low), project_weight[layer].astype(low), expand_weight[layer].astype(low)]
            + [
                contract_weight[layer, at : at + row_share].astype(low)
                for at in range(0, hidden_share, row_share)
            ],
            axis=1,
        )
        for layer in range(layers)
    ]
    mixed_all = []
    for layer in range(layers):
        mixed_all.append(lax.all_gather(mixed_share[layer], BOTH, axis=0, tiled=True))
    small_all, mixed_all[0] = (
        mixed_all[0][:, : position_lanes + vector_lanes],
        mixed_all[0][:, position_lanes + vector_lanes :],
    )
    contract_at = 4 * width + hidden_width
    contract_all = [
        jnp.stack(
            [
                share[:, contract_at + at * width : contract_at + (at + 1) * width].reshape(
                    devices, row_share, width
                )
                for at in range(fold)
            ],
            axis=1,
        ).reshape(hidden_width, width)
        for share in mixed_all
    ]
    attend_all = [share[:, : 3 * width] for share in mixed_all]
    project_all = [share[:, 3 * width : 4 * width] for share in mixed_all]
    expand_all = [share[:, 4 * width : contract_at] for share in mixed_all]
    position_all = small_all[:, :position_lanes].reshape(-1, width)
    vectors_f = (
        small_all[:, position_lanes:].reshape(devices, -1)[:, :vector_share].reshape(-1).astype(jnp.float32)
    )

    turns = jnp.max(heard_first[:, slots_each]) // slots_each + 1
    embedded = looked_up(0, heard_first)
    _, embedded = lax.while_loop(
        lambda carry: carry[0] < turns,
        lambda carry: (carry[0] + 1, carry[1] + looked_up(carry[0], requests(carry[0]))),
        (jnp.int32(1), embedded),
    )

    order = me ^ relative_offsets()
    marks = jnp.take(heard_first[:, slots_each + 1 :].reshape(devices, 2, -1), order, axis=0)
    target_local = marks[:, 0].reshape(-1) - me * rows_each
    valid = marks[:, 1].reshape(-1).astype(jnp.float32)

    hit = jnp.arange(rows_each, dtype=jnp.int32)[None, :] == target_local[:, None]
    target_rows = jnp.dot(hit.astype(low), table_b, preferred_element_type=jnp.float32).astype(low)
    embedded, target_rows = lax.optimization_barrier((embedded, target_rows))

    placed = [positions_of(doc_lengths[micro, 0], doc_order[micro, 0], slot) for micro in range(micro_count)]
    position = jnp.concatenate([pair[0] for pair in placed])
    document = jnp.stack([pair[1] for pair in placed])
    stored = jnp.arange(slot, dtype=jnp.int32)
    position_hot = (position[:, None] == stored[None, :]).astype(low)
    state = embedded + jnp.dot(position_hot, position_all, preferred_element_type=jnp.float32)

    saved = []
    for layer in range(layers):
        (
            gain_one,
            bias_one,
            query_bias,
            value_bias,
            project_bias,
            gain_two,
            bias_two,
            contract_bias,
            expand_bias,
        ) = layer_pieces(vectors_f, layer * block, width, hidden_width)
        normed, scaled_one, inverse_one = norm_forward(state, gain_one, bias_one)
        normed_b = normed.astype(low)
        mixed = jnp.dot(
            normed_b, attend_all[layer], preferred_element_type=jnp.float32
        ) + jnp.concatenate([query_bias, jnp.zeros_like(query_bias), value_bias])
        mixed_b = mixed.astype(low)
        attended_b, log_total = attend_forward(mixed_b, document)
        middle = (
            state
            + jnp.dot(attended_b, project_all[layer], preferred_element_type=jnp.float32)
            + project_bias
        )
        normed_two, scaled_two, inverse_two = norm_forward(middle, gain_two, bias_two)
        normed_two_b = normed_two.astype(low)
        before = (
            jnp.dot(normed_two_b, expand_all[layer], preferred_element_type=jnp.float32)
            + expand_bias
        )
        active_b = gelu_tanh(before).astype(low)
        state = (
            middle
            + jnp.dot(active_b, contract_all[layer], preferred_element_type=jnp.float32)
            + contract_bias
        )
        saved.append(
            (
                normed_b,
                scaled_one,
                inverse_one,
                mixed_b,
                log_total,
                attended_b,
                scaled_two,
                inverse_two,
                normed_two_b,
                before,
                active_b,
            )
        )

    top = layers * block
    final_gain = vectors_f[top : top + width]
    final_bias = vectors_f[top + width : top + 2 * width]
    slots = (loss_slots[:, 0] + slot * jnp.arange(micro_count, dtype=jnp.int32)[:, None]).reshape(-1)
    final, scaled_final, inverse_final = norm_forward(
        jnp.take(state, slots, axis=0), final_gain, final_bias
    )
    rows_all = gather_rows(final.astype(low))
    logits = times_transpose(rows_all, table_b)
    peak = jnp.max(logits, axis=1)
    raised = jnp.exp(logits - peak[:, None])
    totals = jnp.sum(raised, axis=1)
    soft_rows = jnp.dot(raised.astype(low), table_b, preferred_element_type=jnp.float32)
    chosen = jnp.sum(jnp.where(hit, logits, 0.0), axis=1)
    stats = jnp.stack([peak.reshape(devices, -1), totals.reshape(devices, -1)], axis=1)
    inverse = jnp.argsort(order)
    stats_all = spread(jnp.take(stats, inverse, axis=0).reshape(devices, -1))
    stats_all = stats_all.reshape(devices, devices, 2, -1)
    peak_all = jnp.max(stats_all[:, :, 0], axis=0)
    totals_all = jnp.sum(stats_all[:, :, 1] * jnp.exp(stats_all[:, :, 0] - peak_all[None]), axis=0)
    log_rows = jnp.take(peak_all + jnp.log(totals_all), order, axis=0).reshape(-1)
    own = micro_count * loss_rows
    entropy_local = jnp.sum(log_rows[:own] * valid[:own]) - jnp.sum(chosen * valid)
    grad_logits = (
        (jnp.exp(logits - log_rows[:, None]) - hit.astype(jnp.float32)) * valid[:, None]
    ).astype(low)
    share_rows = jnp.exp(peak - log_rows) * valid
    grad_final = scatter_rows(
        share_rows[:, None] * soft_rows - valid[:, None] * target_rows.astype(jnp.float32)
    )
    table_grad = outer_sum(grad_logits, rows_all)
    grad_final, table_grad = lax.optimization_barrier((grad_final, table_grad))
    grad_rows, grad_final_gain, grad_final_bias = norm_backward(
        grad_final, scaled_final, inverse_final, final_gain
    )
    slot_hot = (jnp.arange(tokens, dtype=jnp.int32)[:, None] == slots[None, :]).astype(jnp.float32)
    grad_state = jnp.dot(slot_hot, grad_rows, precision=lax.Precision.HIGHEST)

    layer_grads = [None] * layers
    wide_sent, narrow_sent = [None] * layers, [None] * layers
    for layer in reversed(range(layers)):
        (
            normed_b,
            scaled_one,
            inverse_one,
            mixed_b,
            log_total,
            attended_b,
            scaled_two,
            inverse_two,
            normed_two_b,
            before,
            active_b,
        ) = saved[layer]
        gain_one, _, _, _, _, gain_two, _, _, _ = layer_pieces(vectors_f, layer * block, width, hidden_width)
        grad_out = grad_state.astype(low)
        contract_grad = outer_sum(active_b, grad_out).astype(low)
        grad_contract_bias = jnp.sum(grad_out.astype(jnp.float32), axis=0)
        grad_active = times_transpose(grad_out, contract_all[layer])
        grad_before = (grad_active * gelu_slope(before)).astype(low)
        expand_grad = outer_sum(normed_two_b, grad_before).astype(low)
        wide_sent[layer] = send_core(
            [contract_grad.reshape(devices, hidden_share, width)]
            + lanes_to_rows(expand_grad, devices, width)
        )
        grad_expand_bias = jnp.sum(grad_before.astype(jnp.float32), axis=0)
        grad_normed_two = times_transpose(grad_before, expand_all[layer])
        grad_mid, grad_gain_two, grad_bias_two = norm_backward(
            grad_normed_two, scaled_two, inverse_two, gain_two
        )
        grad_middle = grad_state + grad_mid
        grad_project = grad_middle.astype(low)
        wide_sent[layer] = send_quads(wide_sent[layer])
        project_grad = outer_sum(attended_b, grad_project).astype(low)
        grad_project_bias = jnp.sum(grad_project.astype(jnp.float32), axis=0)
        grad_attended = times_transpose(grad_project, project_all[layer]).astype(low)
        if layer < layers - 1:
            wide_sent[layer + 1] = send_deep(wide_sent[layer + 1])
        grad_mixed = attend_backward(mixed_b, document, log_total, grad_attended)
        attend_grad = outer_sum(normed_b, grad_mixed).astype(low)
        grad_mixed_f = grad_mixed.astype(jnp.float32)
        grad_query_bias = jnp.sum(grad_mixed_f[:, :width], axis=0)
        grad_value_bias = jnp.sum(grad_mixed_f[:, 2 * width :], axis=0)
        grad_normed = times_transpose(grad_mixed, attend_all[layer])
        grad_in, grad_gain_one, grad_bias_one = norm_backward(
            grad_normed, scaled_one, inverse_one, gain_one
        )
        grad_state = grad_middle + grad_in
        layer_grads[layer] = jnp.concatenate(
            [
                grad_gain_one,
                grad_bias_one,
                grad_query_bias,
                grad_value_bias,
                grad_project_bias,
                grad_gain_two,
                grad_bias_two,
                grad_contract_bias,
                grad_expand_bias,
            ]
        )

        narrow = lanes_to_rows(attend_grad, devices, width) + lanes_to_rows(project_grad, devices, width)
        if layer == 0:
            grad_embedded = grad_state.astype(low)
            position_grad = outer_sum(position_hot, grad_embedded).astype(low)
            vector_grad = jnp.concatenate(layer_grads + [grad_final_gain, grad_final_bias]).astype(low)
            vector_grad = jnp.pad(
                vector_grad.reshape(devices, vector_share),
                ((0, 0), (0, (small_rows - position_share) * width - vector_share)),
            )
            small_grad = [
                position_grad.reshape(devices, position_share, width),
                vector_grad.reshape(devices, small_rows - position_share, width),
            ]
            narrow = narrow + [jnp.concatenate(small_grad, axis=1)]
        narrow_sent[layer] = send_core(narrow)
        narrow_sent[layer] = send_quads(narrow_sent[layer])

    def returned(turn):
        return outer_sum(seat_matrix(turn), grad_embedded).astype(low).reshape(devices, slots_each, width)

    came = lax.all_to_all(returned(0), BOTH, 0, 0, tiled=True)
    table_grad = table_grad + outer_sum(wanted_of(heard_first), came.reshape(slots_all, width))

    def later_turn(carry):
        turn, total = carry
        rows = lax.all_to_all(returned(turn), BOTH, 0, 0, tiled=True).reshape(slots_all, width)
        return (turn + 1, total + outer_sum(wanted_of(requests(turn)), rows))

    _, table_sum = lax.while_loop(lambda carry: carry[0] < turns, later_turn, (jnp.int32(1), table_grad))
    for layer in range(1, layers):
        narrow_sent[layer] = send_deep(narrow_sent[layer])
    wide_sent[0] = send_deep(wide_sent[0])
    narrow_sent[0] = send_deep(narrow_sent[0])
    wide_sums = [sum_low(sent) for sent in wide_sent]
    narrow_sums = [sum_low(sent) for sent in narrow_sent]

    contract_sum = jnp.stack([total[:hidden_share] for total in wide_sums])
    expand_sum = jnp.stack(
        [rows_to_lanes(total[hidden_share:], hidden_width // width) for total in wide_sums]
    )
    attend_sum = jnp.stack([rows_to_lanes(total[: 3 * row_share], 3) for total in narrow_sums])
    project_sum = jnp.stack([total[3 * row_share : 4 * row_share] for total in narrow_sums])
    small_sum = narrow_sums[0][4 * row_share :]
    position_sum = small_sum[:position_share]
    vector_sum = small_sum[position_share : position_share + vector_rows].reshape(-1)[:vector_share]

    sums = (table_sum, position_sum, attend_sum, project_sum, expand_sum, contract_sum, vector_sum)
    squares = jnp.zeros((), jnp.float32)
    for grad in sums:
        squares = squares + jnp.sum(grad * grad)
    scalars = jnp.stack([squares, entropy_local, jnp.sum(loss_mask).astype(jnp.float32)])
    square_total, entropy_total, count = jnp.sum(spread(scalars).reshape(devices, 3), axis=0)
    grad_norm = jnp.sqrt(square_total) / count
    factor = clip_limit / jnp.maximum(grad_norm, clip_limit)
    loss = entropy_total / count
    weights = (
        token_table,
        position_table,
        attend_weight,
        project_weight,
        expand_weight,
        contract_weight,
        vector_params,
    )
    moments = (
        table_moments,
        position_moments,
        attend_moments,
        project_moments,
        expand_moments,
        contract_moments,
        vector_moments,
    )
    decays = (decay_rate, decay_rate, decay_rate, decay_rate, decay_rate, decay_rate, 0.0)

    def updated(weight, moment, grad, decay):
        if weight.ndim < 2:
            return adam_update(weight, moment, grad / count * factor, decay)
        lanes = weight.shape[-1]
        fresh, pair, copy = adam_blocks(
            weight.reshape(-1, lanes), moment.reshape(2, -1, lanes), grad.reshape(-1, lanes), count, factor, decay
        )
        return (fresh.reshape(weight.shape), pair.reshape(moment.shape), copy.reshape(weight.shape))

    table_new, position_new, attend_new, project_new, expand_new, contract_new, vector_new = [
        updated(weight, moment, grad, decay)
        for weight, moment, grad, decay in zip(weights, moments, sums, decays)
    ]
    return (
        loss,
        grad_norm,
        table_new[0],
        position_new[0],
        attend_new[0],
        project_new[0],
        expand_new[0],
        contract_new[0],
        vector_new[0],
        table_new[1],
        position_new[1],
        attend_new[1],
        project_new[1],
        expand_new[1],
        contract_new[1],
        vector_new[1],
        table_new[2],
        position_new[2],
        attend_new[2],
        project_new[2],
        expand_new[2],
        contract_new[2],
        vector_new[2],
    )


def solution(mesh):
    return jax.shard_map(
        shards,
        mesh=mesh,
        in_specs=(
            P(None, ("dp", "fsdp"), None),
            P(None, ("dp", "fsdp"), None),
            P(None, ("dp", "fsdp"), None),
            P(None, ("dp", "fsdp"), None),
            P(None, ("dp", "fsdp"), None),
            P(None, ("dp", "fsdp"), None),
            P(("dp", "fsdp"), None),
            P(("dp", "fsdp"), None),
            P(None, ("dp", "fsdp"), None),
            P(None, ("dp", "fsdp"), None),
            P(None, ("dp", "fsdp"), None),
            P(None, ("dp", "fsdp"), None),
            P(("dp", "fsdp")),
            P(None, ("dp", "fsdp"), None),
            P(None, ("dp", "fsdp"), None),
            P(None, None, ("dp", "fsdp"), None),
            P(None, None, ("dp", "fsdp"), None),
            P(None, None, ("dp", "fsdp"), None),
            P(None, None, ("dp", "fsdp"), None),
            P(None, ("dp", "fsdp")),
        ),
        out_specs=(
            P(),
            P(),
            P(("dp", "fsdp"), None),
            P(("dp", "fsdp"), None),
            P(None, ("dp", "fsdp"), None),
            P(None, ("dp", "fsdp"), None),
            P(None, ("dp", "fsdp"), None),
            P(None, ("dp", "fsdp"), None),
            P(("dp", "fsdp")),
            P(None, ("dp", "fsdp"), None),
            P(None, ("dp", "fsdp"), None),
            P(None, None, ("dp", "fsdp"), None),
            P(None, None, ("dp", "fsdp"), None),
            P(None, None, ("dp", "fsdp"), None),
            P(None, None, ("dp", "fsdp"), None),
            P(None, ("dp", "fsdp")),
            P(("dp", "fsdp"), None),
            P(("dp", "fsdp"), None),
            P(None, ("dp", "fsdp"), None),
            P(None, ("dp", "fsdp"), None),
            P(None, ("dp", "fsdp"), None),
            P(None, ("dp", "fsdp"), None),
            P(("dp", "fsdp")),
        ),
        check_vma=False,
    )
```

```python
import functools

import jax
import jax.numpy as jnp
from jax import lax
from jax.experimental import pallas as pl
from jax.experimental.pallas import tpu as pltpu
from jax.sharding import PartitionSpec as P

HEADS = 12


norm_eps = 1e-05
gelu_scale = 0.7978845608
gelu_cubic = 0.044715
beta_one = 0.5
beta_two = 0.5
learn_rate = 0.03
decay_rate = 0.1
adam_eps = 1e-08
clip_limit = 0.25
adam_step = 3
masked_score = -1e30


def positions_of(lengths, order, slot):
    places = jnp.arange(lengths.shape[0], dtype=jnp.int32)
    place = jnp.sum(places[None, :] * (order[None, :] == places[:, None]).astype(jnp.int32), axis=1)
    offset = jnp.sum(lengths[None, :] * (place[None, :] < place[:, None]).astype(jnp.int32), axis=1)
    ends = jnp.cumsum(lengths)
    starts = ends - lengths
    stored = jnp.arange(slot, dtype=jnp.int32)
    document = jnp.sum((stored[:, None] >= ends[None, :]).astype(jnp.int32), axis=1)
    onehot = (document[:, None] == places[None, :]).astype(jnp.int32)
    position = stored + jnp.sum(onehot * (offset - starts)[None, :], axis=1)
    return (position, document)


def norm_forward(state, gain, bias):
    average = jnp.mean(state, axis=-1, keepdims=True)
    centered = state - average
    inverse = lax.rsqrt(jnp.mean(centered * centered, axis=-1, keepdims=True) + norm_eps)
    scaled = centered * inverse
    return (scaled * gain + bias, scaled, inverse)


def norm_backward(grad, scaled, inverse, gain):
    shaped = grad * gain
    inner = (
        shaped
        - jnp.mean(shaped, axis=-1, keepdims=True)
        - scaled * jnp.mean(shaped * scaled, axis=-1, keepdims=True)
    )
    return (inner * inverse, jnp.sum(grad * scaled, axis=0), jnp.sum(grad, axis=0))


def gelu_tanh(value):
    return 0.5 * value * (1.0 + jnp.tanh(gelu_scale * (value + gelu_cubic * value * value * value)))


def gelu_slope(value):
    bent = jnp.tanh(gelu_scale * (value + gelu_cubic * value * value * value))
    return 0.5 * (1.0 + bent) + 0.5 * value * (1.0 - bent * bent) * gelu_scale * (
        1.0 + 3.0 * gelu_cubic * value * value
    )


def outer_sum(left, right):
    return lax.dot_general(
        left, right, (((0,), (0,)), ((), ())), preferred_element_type=jnp.float32
    )


def times_transpose(left, right):
    return lax.dot_general(
        left, right, (((1,), (1,)), ((), ())), preferred_element_type=jnp.float32
    )


BOTH = ("dp", "fsdp")


def swapped(value, axis, flip):
    size = lax.axis_size(axis)
    return lax.ppermute(value, axis, [(index, index ^ flip) for index in range(size)])


def spread(value):
    count = lax.axis_size("dp") * lax.axis_size("fsdp")
    return lax.all_to_all(jnp.broadcast_to(value[None], (count,) + value.shape), BOTH, 0, 0, tiled=True)


def relative_offsets():
    quads, fsdp = lax.axis_size("dp") // 2, lax.axis_size("fsdp")
    return jnp.array(
        [
            (quad * 2 + core) * fsdp + deep
            for core in range(2)
            for quad in range(quads)
            for deep in range(fsdp)
        ],
        jnp.int32,
    )


def gather_rows(rows):
    quads, fsdp = lax.axis_size("dp") // 2, lax.axis_size("fsdp")
    held = jnp.stack([rows] + [swapped(rows, "fsdp", flip) for flip in range(1, fsdp)])
    held = jnp.stack([held] + [swapped(held, "dp", 2 * flip) for flip in range(1, quads)])
    held = jnp.stack([held, swapped(held, "dp", 1)])
    return held.reshape((-1,) + rows.shape[1:])


def sum_low(pieces):
    total = pieces[0].astype(jnp.float32)
    for piece in pieces[1:]:
        total = total + piece.astype(jnp.float32)
    return total


def head_quads(value, flip):
    return swapped(value, "dp", 2 * flip)


def scatter_rows(partial):
    quads, fsdp = lax.axis_size("dp") // 2, lax.axis_size("fsdp")
    width = partial.shape[1]
    part = partial.astype(jnp.bfloat16).reshape(2, quads, fsdp, -1, width)
    part = sum_low([part[0], swapped(part[1], "dp", 1)]).astype(jnp.bfloat16)
    part = sum_low(
        [part[0]] + [head_quads(part[flip], flip) for flip in range(1, quads)]
    ).astype(jnp.bfloat16)
    return sum_low([part[0]] + [swapped(part[flip], "fsdp", flip) for flip in range(1, fsdp)])


def take_one(value, index, axis):
    return lax.dynamic_index_in_dim(value, index, axis, keepdims=False)


def send_core(pieces):
    quads, fsdp = lax.axis_size("dp") // 2, lax.axis_size("fsdp")
    core = lax.axis_index("dp") % 2
    views = [piece.reshape((quads, 2, fsdp) + piece.shape[1:]) for piece in pieces]

    def half(which):
        return jnp.concatenate([take_one(view, which, 1) for view in views], axis=2)

    return [half(core), swapped(half(1 - core), "dp", 1)]


def send_quads(parts):
    quads = lax.axis_size("dp") // 2
    quad = lax.axis_index("dp") // 2
    part = sum_low(parts).astype(jnp.bfloat16)
    return [take_one(part, quad, 0)] + [
        swapped(take_one(part, quad ^ flip, 0), "dp", 2 * flip) for flip in range(1, quads)
    ]


def send_deep(parts):
    fsdp, deep = lax.axis_size("fsdp"), lax.axis_index("fsdp")
    part = sum_low(parts).astype(jnp.bfloat16)
    return [take_one(part, deep, 0)] + [
        swapped(take_one(part, deep ^ flip, 0), "fsdp", flip) for flip in range(1, fsdp)
    ]


def lanes_to_rows(value, devices, width):
    view = value.reshape(devices, -1, value.shape[1])
    return [view[:, :, at : at + width] for at in range(0, value.shape[1], width)]


def rows_to_lanes(value, parts):
    rows = value.shape[0] // parts
    return jnp.concatenate([value[index * rows : (index + 1) * rows] for index in range(parts)], axis=1)


def dotted(left, right, left_at, right_at):
    return lax.dot_general(
        left, right, (((left_at,), (right_at,)), ((), ())), preferred_element_type=jnp.float32
    )


def allowed_of(row_ref, column_ref):
    slot = row_ref.shape[2]
    here = lax.broadcasted_iota(jnp.int32, (slot, slot), 0)
    there = lax.broadcasted_iota(jnp.int32, (slot, slot), 1)
    return (column_ref[0] == row_ref[0]) & (there <= here)


def attend_kernel(head, row_ref, column_ref, mixed_ref, attended_ref, log_ref):
    slot, width = attended_ref.shape
    allowed = allowed_of(row_ref, column_ref)
    for base in range(0, width, 2 * head):
        query, keys, values = [
            mixed_ref[:, part * width + base : part * width + base + 2 * head] for part in range(3)
        ]
        results, logs = [], []
        for at in (0, head):
            raw = dotted(query[:, at : at + head], keys[:, at : at + head], 1, 1)
            scores = jnp.where(allowed, raw * head ** (-0.5), masked_score)
            peak = jnp.max(scores, axis=1, keepdims=True)
            log_total = peak + jnp.log(jnp.sum(jnp.exp(scores - peak), axis=1, keepdims=True))
            probs = jnp.exp(scores - log_total).astype(jnp.bfloat16)
            results.append(dotted(probs, values[:, at : at + head], 1, 0))
            logs.append(jnp.broadcast_to(log_total, (slot, head)))
        attended_ref[:, base : base + 2 * head] = jnp.concatenate(results, axis=1).astype(jnp.bfloat16)
        log_ref[:, base : base + 2 * head] = jnp.concatenate(logs, axis=1)


def attend_back_kernel(head, row_ref, column_ref, mixed_ref, log_ref, grad_ref, out_ref):
    width = grad_ref.shape[1]
    allowed = allowed_of(row_ref, column_ref)
    scale = head ** (-0.5)
    for base in range(0, width, 2 * head):
        query, keys, values = [
            mixed_ref[:, part * width + base : part * width + base + 2 * head] for part in range(3)
        ]
        grads = grad_ref[:, base : base + 2 * head]
        logs = log_ref[:, base : base + 2 * head]
        parts = [[], [], []]
        for at in (0, head):
            q, k, v, g = [value[:, at : at + head] for value in (query, keys, values, grads)]
            scores = jnp.where(allowed, dotted(q, k, 1, 1) * scale, masked_score)
            probs = jnp.exp(scores - logs[:, at : at + 1])
            parts[2].append(dotted(probs.astype(jnp.bfloat16), g, 0, 0))
            slopes = dotted(g, v, 1, 1)
            slopes = probs * (slopes - jnp.sum(probs * slopes, axis=1, keepdims=True))
            slopes = (slopes * scale).astype(jnp.bfloat16)
            parts[0].append(dotted(slopes, k, 1, 0))
            parts[1].append(dotted(slopes, q, 0, 0))
        for which in range(3):
            out_ref[:, which * width + base : which * width + base + 2 * head] = jnp.concatenate(
                parts[which], axis=1
            ).astype(jnp.bfloat16)


def attend_specs(document, width):
    _, slot = document.shape
    return [
        pl.BlockSpec((1, 1, slot), lambda m: (m, 0, 0)),
        pl.BlockSpec((1, slot, 1), lambda m: (m, 0, 0)),
        pl.BlockSpec((slot, 3 * width), lambda m: (m, 0)),
    ], pl.BlockSpec((slot, width), lambda m: (m, 0))


def attend_cost(document, width, dots):
    micro, slot = document.shape
    return pl.CostEstimate(
        flops=2 * dots * micro * slot * slot * width,
        transcendentals=2 * micro * slot * slot * HEADS,
        bytes_accessed=16 * micro * slot * width,
    )


def attend_forward(mixed, document):
    rows, width = mixed.shape[0], mixed.shape[1] // 3
    specs, thin = attend_specs(document, width)
    return pl.pallas_call(
        functools.partial(attend_kernel, width // HEADS),
        grid=(document.shape[0],),
        in_specs=specs,
        out_specs=[thin, thin],
        out_shape=[
            jax.ShapeDtypeStruct((rows, width), jnp.bfloat16),
            jax.ShapeDtypeStruct((rows, width), jnp.float32),
        ],
        cost_estimate=attend_cost(document, width, 2),
        name="attend_forward",
    )(document[:, None, :], document[:, :, None], mixed)


def attend_backward(mixed, document, log_total, grad_attended):
    width = mixed.shape[1] // 3
    specs, thin = attend_specs(document, width)
    return pl.pallas_call(
        functools.partial(attend_back_kernel, width // HEADS),
        grid=(document.shape[0],),
        in_specs=specs + [thin, thin],
        out_specs=specs[2],
        out_shape=jax.ShapeDtypeStruct(mixed.shape, jnp.bfloat16),
        cost_estimate=attend_cost(document, width, 5),
        name="attend_backward",
    )(document[:, None, :], document[:, :, None], mixed, log_total, grad_attended)


def layer_pieces(vectors, base, width, hidden_width):
    pieces = [vectors[base + index * width : base + (index + 1) * width] for index in range(8)]
    return pieces + [vectors[base + 8 * width : base + 8 * width + hidden_width]]


def adam_update(weight, moments, grad, decay):
    first = beta_one * moments[0] + (1.0 - beta_one) * grad
    root = jnp.sqrt(beta_two * moments[1] * moments[1] + (1.0 - beta_two) * grad * grad)
    rise = (
        first / (1.0 - beta_one**adam_step) / (root / (1.0 - beta_two**adam_step) ** 0.5 + adam_eps)
    )
    fresh = weight - learn_rate * (rise + decay * weight)
    return (fresh, jnp.stack([first, root]), fresh.astype(jnp.bfloat16))


def adam_kernel(decay, scale_ref, weight_ref, moments_ref, grad_ref, fresh_ref, state_ref, copy_ref):
    fresh, state, copy = adam_update(
        weight_ref[...], moments_ref[...], grad_ref[...] / scale_ref[0] * scale_ref[1], decay
    )
    fresh_ref[...], state_ref[...], copy_ref[...] = fresh, state, copy


def adam_blocks(weight, moments, grad, count, factor, decay):
    rows, width = weight.shape
    step = rows if rows <= 320 else max(size for size in range(16, 161, 16) if rows % size == 0)
    flat = pl.BlockSpec((step, width), lambda at: (at, 0))
    pair = pl.BlockSpec((2, step, width), lambda at: (0, at, 0))
    return pl.pallas_call(
        functools.partial(adam_kernel, decay),
        grid=(rows // step,),
        in_specs=[pl.BlockSpec(memory_space=pltpu.SMEM), flat, pair, flat],
        out_specs=[flat, pair, flat],
        out_shape=[
            jax.ShapeDtypeStruct(weight.shape, jnp.float32),
            jax.ShapeDtypeStruct(moments.shape, jnp.float32),
            jax.ShapeDtypeStruct(weight.shape, jnp.bfloat16),
        ],
        cost_estimate=pl.CostEstimate(
            flops=20 * rows * width, transcendentals=rows * width, bytes_accessed=30 * rows * width
        ),
        name="adam_blocks",
    )(jnp.stack([count, factor]), weight, moments, grad)


def shards(
    token_ids,
    doc_lengths,
    doc_order,
    loss_slots,
    targets,
    loss_mask,
    token_table,
    position_table,
    attend_weight,
    project_weight,
    expand_weight,
    contract_weight,
    vector_params,
    table_moments,
    position_moments,
    attend_moments,
    project_moments,
    expand_moments,
    contract_moments,
    vector_moments,
):
    low = jnp.bfloat16
    fsdp = lax.axis_size("fsdp")
    devices = lax.axis_size("dp") * fsdp
    me = lax.axis_index("dp") * fsdp + lax.axis_index("fsdp")
    micro_count, _, slot = token_ids.shape
    loss_rows = loss_slots.shape[2]
    tokens = micro_count * slot
    width = token_table.shape[1]
    layers, row_share = attend_weight.shape[:2]
    hidden_width = expand_weight.shape[2]
    hidden_share = contract_weight.shape[1]
    rows_each = token_table.shape[0]
    position_share = position_table.shape[0]
    vector_share = vector_params.shape[0]
    block = 8 * width + hidden_width
    vector_rows = -(-vector_share // width)
    small_rows = -(-(position_share + vector_rows) // 16) * 16

    words = token_ids.reshape(tokens)
    owner = words // rows_each
    local = words % rows_each
    earlier = jnp.arange(tokens)[None, :] < jnp.arange(tokens)[:, None]
    first = jnp.logical_not(jnp.any((words[:, None] == words[None, :]) & earlier, axis=1))
    rank = jnp.sum(
        (first[None, :] & (owner[:, None] == owner[None, :]) & (words[None, :] < words[:, None])).astype(jnp.int32),
        axis=1,
    )
    slots_each = max(16, 2 * tokens // devices)
    slots_all = devices * slots_each

    def seats(turn):
        within = rank - turn * slots_each
        return jnp.where((within >= 0) & (within < slots_each), owner * slots_each + within, -1)

    def requests(turn, *marks):
        seat = seats(turn)
        asked = jnp.max(
            jnp.where(seat[None, :] == jnp.arange(slots_all)[:, None], local[None, :], -1), axis=1
        )
        table = jnp.concatenate(
            [asked.reshape(devices, slots_each), jnp.broadcast_to(jnp.max(rank), (devices, 1))]
            + [jnp.broadcast_to(mark.reshape(1, -1), (devices, mark.size)) for mark in marks],
            axis=1,
        )
        return lax.all_to_all(table, BOTH, 0, 0, tiled=True)

    def wanted_of(heard):
        asked = heard[:, :slots_each].reshape(-1)
        return (asked[:, None] == jnp.arange(rows_each)[None, :]).astype(low)

    def seat_matrix(turn):
        return (seats(turn)[:, None] == jnp.arange(slots_all)[None, :]).astype(low)

    table_b = token_table.astype(low)

    def looked_up(turn, heard):
        rows = jnp.dot(wanted_of(heard), table_b, preferred_element_type=jnp.float32).astype(low)
        rows = lax.all_to_all(rows, BOTH, 0, 0, tiled=True)
        return jnp.dot(seat_matrix(turn), rows, preferred_element_type=jnp.float32)

    heard_first = requests(0, targets, loss_mask)
    fold = hidden_share // row_share
    position_lanes = position_share * width // row_share
    vector_lanes = 128 * -(-vector_share // (128 * row_share))
    small = [
        position_table.astype(low).reshape(row_share, position_lanes),
        jnp.pad(vector_params.astype(low), (0, row_share * vector_lanes - vector_share)).reshape(
            row_share, vector_lanes
        ),
    ]
    mixed_share = [
        jnp.concatenate(
            (small if layer == 0 else [])
            + [attend_weight[layer].astype(low), project_weight[layer].astype(low), expand_weight[layer].astype(low)]
            + [
                contract_weight[layer, at : at + row_share].astype(low)
                for at in range(0, hidden_share, row_share)
            ],
            axis=1,
        )
        for layer in range(layers)
    ]
    mixed_all = []
    for layer in range(layers):
        mixed_all.append(lax.all_gather(mixed_share[layer], BOTH, axis=0, tiled=True))
    small_all, mixed_all[0] = (
        mixed_all[0][:, : position_lanes + vector_lanes],
        mixed_all[0][:, position_lanes + vector_lanes :],
    )
    contract_at = 4 * width + hidden_width
    contract_all = [
        jnp.stack(
            [
                share[:, contract_at + at * width : contract_at + (at + 1) * width].reshape(
                    devices, row_share, width
                )
                for at in range(fold)
            ],
            axis=1,
        ).reshape(hidden_width, width)
        for share in mixed_all
    ]
    attend_all = [share[:, : 3 * width] for share in mixed_all]
    project_all = [share[:, 3 * width : 4 * width] for share in mixed_all]
    expand_all = [share[:, 4 * width : contract_at] for share in mixed_all]
    position_all = small_all[:, :position_lanes].reshape(-1, width)
    vectors_f = (
        small_all[:, position_lanes:].reshape(devices, -1)[:, :vector_share].reshape(-1).astype(jnp.float32)
    )

    turns = jnp.max(heard_first[:, slots_each]) // slots_each + 1
    embedded = looked_up(0, heard_first)
    _, embedded = lax.while_loop(
        lambda carry: carry[0] < turns,
        lambda carry: (carry[0] + 1, carry[1] + looked_up(carry[0], requests(carry[0]))),
        (jnp.int32(1), embedded),
    )

    order = me ^ relative_offsets()
    marks = jnp.take(heard_first[:, slots_each + 1 :].reshape(devices, 2, -1), order, axis=0)
    target_local = marks[:, 0].reshape(-1) - me * rows_each
    valid = marks[:, 1].reshape(-1).astype(jnp.float32)

    hit = jnp.arange(rows_each, dtype=jnp.int32)[None, :] == target_local[:, None]
    target_rows = jnp.dot(hit.astype(low), table_b, preferred_element_type=jnp.float32).astype(low)
    embedded, target_rows = lax.optimization_barrier((embedded, target_rows))

    placed = [positions_of(doc_lengths[micro, 0], doc_order[micro, 0], slot) for micro in range(micro_count)]
    position = jnp.concatenate([pair[0] for pair in placed])
    document = jnp.stack([pair[1] for pair in placed])
    stored = jnp.arange(slot, dtype=jnp.int32)
    position_hot = (position[:, None] == stored[None, :]).astype(low)
    state = embedded + jnp.dot(position_hot, position_all, preferred_element_type=jnp.float32)

    saved = []
    for layer in range(layers):
        (
            gain_one,
            bias_one,
            query_bias,
            value_bias,
            project_bias,
            gain_two,
            bias_two,
            contract_bias,
            expand_bias,
        ) = layer_pieces(vectors_f, layer * block, width, hidden_width)
        normed, scaled_one, inverse_one = norm_forward(state, gain_one, bias_one)
        normed_b = normed.astype(low)
        mixed = jnp.dot(
            normed_b, attend_all[layer], preferred_element_type=jnp.float32
        ) + jnp.concatenate([query_bias, jnp.zeros_like(query_bias), value_bias])
        mixed_b = mixed.astype(low)
        attended_b, log_total = attend_forward(mixed_b, document)
        middle = (
            state
            + jnp.dot(attended_b, project_all[layer], preferred_element_type=jnp.float32)
            + project_bias
        )
        normed_two, scaled_two, inverse_two = norm_forward(middle, gain_two, bias_two)
        normed_two_b = normed_two.astype(low)
        before = (
            jnp.dot(normed_two_b, expand_all[layer], preferred_element_type=jnp.float32)
            + expand_bias
        )
        active_b = gelu_tanh(before).astype(low)
        state = (
            middle
            + jnp.dot(active_b, contract_all[layer], preferred_element_type=jnp.float32)
            + contract_bias
        )
        saved.append(
            (
                normed_b,
                scaled_one,
                inverse_one,
                mixed_b,
                log_total,
                attended_b,
                scaled_two,
                inverse_two,
                normed_two_b,
                before,
                active_b,
            )
        )

    top = layers * block
    final_gain = vectors_f[top : top + width]
    final_bias = vectors_f[top + width : top + 2 * width]
    slots = (loss_slots[:, 0] + slot * jnp.arange(micro_count, dtype=jnp.int32)[:, None]).reshape(-1)
    final, scaled_final, inverse_final = norm_forward(
        jnp.take(state, slots, axis=0), final_gain, final_bias
    )
    rows_all = gather_rows(final.astype(low))
    logits = times_transpose(rows_all, table_b)
    peak = jnp.max(logits, axis=1)
    raised = jnp.exp(logits - peak[:, None])
    totals = jnp.sum(raised, axis=1)
    soft_rows = lax.optimization_barrier(
        jnp.dot(raised.astype(low), table_b, preferred_element_type=jnp.float32)
    )
    chosen = jnp.sum(jnp.where(hit, logits, 0.0), axis=1)
    stats = jnp.stack([peak.reshape(devices, -1), totals.reshape(devices, -1)], axis=1)
    inverse = jnp.argsort(order)
    stats_all = spread(jnp.take(stats, inverse, axis=0).reshape(devices, -1))
    stats_all = stats_all.reshape(devices, devices, 2, -1)
    peak_all = jnp.max(stats_all[:, :, 0], axis=0)
    totals_all = jnp.sum(stats_all[:, :, 1] * jnp.exp(stats_all[:, :, 0] - peak_all[None]), axis=0)
    log_rows = jnp.take(peak_all + jnp.log(totals_all), order, axis=0).reshape(-1)
    own = micro_count * loss_rows
    entropy_local = jnp.sum(log_rows[:own] * valid[:own]) - jnp.sum(chosen * valid)
    grad_logits = (
        (jnp.exp(logits - log_rows[:, None]) - hit.astype(jnp.float32)) * valid[:, None]
    ).astype(low)
    share_rows = jnp.exp(peak - log_rows) * valid
    grad_final = scatter_rows(
        share_rows[:, None] * soft_rows - valid[:, None] * target_rows.astype(jnp.float32)
    )
    table_grad = outer_sum(grad_logits, rows_all)
    grad_final, table_grad = lax.optimization_barrier((grad_final, table_grad))
    grad_rows, grad_final_gain, grad_final_bias = norm_backward(
        grad_final, scaled_final, inverse_final, final_gain
    )
    slot_hot = (jnp.arange(tokens, dtype=jnp.int32)[:, None] == slots[None, :]).astype(jnp.float32)
    grad_state = jnp.dot(slot_hot, grad_rows, precision=lax.Precision.HIGHEST)

    layer_grads = [None] * layers
    wide_sent, narrow_sent = [None] * layers, [None] * layers
    for layer in reversed(range(layers)):
        (
            normed_b,
            scaled_one,
            inverse_one,
            mixed_b,
            log_total,
            attended_b,
            scaled_two,
            inverse_two,
            normed_two_b,
            before,
            active_b,
        ) = saved[layer]
        gain_one, _, _, _, _, gain_two, _, _, _ = layer_pieces(vectors_f, layer * block, width, hidden_width)
        grad_out = grad_state.astype(low)
        contract_grad = outer_sum(active_b, grad_out).astype(low)
        grad_contract_bias = jnp.sum(grad_out.astype(jnp.float32), axis=0)
        grad_active = times_transpose(grad_out, contract_all[layer])
        grad_before = (grad_active * gelu_slope(before)).astype(low)
        expand_grad = outer_sum(normed_two_b, grad_before).astype(low)
        wide_sent[layer] = send_core(
            [contract_grad.reshape(devices, hidden_share, width)]
            + lanes_to_rows(expand_grad, devices, width)
        )
        grad_expand_bias = jnp.sum(grad_before.astype(jnp.float32), axis=0)
        grad_normed_two = times_transpose(grad_before, expand_all[layer])
        grad_mid, grad_gain_two, grad_bias_two = norm_backward(
            grad_normed_two, scaled_two, inverse_two, gain_two
        )
        grad_middle = grad_state + grad_mid
        grad_project = grad_middle.astype(low)
        wide_sent[layer] = send_quads(wide_sent[layer])
        project_grad = outer_sum(attended_b, grad_project).astype(low)
        grad_project_bias = jnp.sum(grad_project.astype(jnp.float32), axis=0)
        grad_attended = times_transpose(grad_project, project_all[layer]).astype(low)
        if layer < layers - 1:
            wide_sent[layer + 1] = send_deep(wide_sent[layer + 1])
        grad_mixed = attend_backward(mixed_b, document, log_total, grad_attended)
        attend_grad = outer_sum(normed_b, grad_mixed).astype(low)
        grad_mixed_f = grad_mixed.astype(jnp.float32)
        grad_query_bias = jnp.sum(grad_mixed_f[:, :width], axis=0)
        grad_value_bias = jnp.sum(grad_mixed_f[:, 2 * width :], axis=0)
        grad_normed = times_transpose(grad_mixed, attend_all[layer])
        grad_in, grad_gain_one, grad_bias_one = norm_backward(
            grad_normed, scaled_one, inverse_one, gain_one
        )
        grad_state = grad_middle + grad_in
        layer_grads[layer] = jnp.concatenate(
            [
                grad_gain_one,
                grad_bias_one,
                grad_query_bias,
                grad_value_bias,
                grad_project_bias,
                grad_gain_two,
                grad_bias_two,
                grad_contract_bias,
                grad_expand_bias,
            ]
        )

        narrow = lanes_to_rows(attend_grad, devices, width) + lanes_to_rows(project_grad, devices, width)
        if layer == 0:
            grad_embedded = grad_state.astype(low)
            position_grad = outer_sum(position_hot, grad_embedded).astype(low)
            vector_grad = jnp.concatenate(layer_grads + [grad_final_gain, grad_final_bias]).astype(low)
            vector_grad = jnp.pad(
                vector_grad.reshape(devices, vector_share),
                ((0, 0), (0, (small_rows - position_share) * width - vector_share)),
            )
            small_grad = [
                position_grad.reshape(devices, position_share, width),
                vector_grad.reshape(devices, small_rows - position_share, width),
            ]
            narrow = narrow + [jnp.concatenate(small_grad, axis=1)]
        narrow_sent[layer] = send_core(narrow)
        narrow_sent[layer] = send_quads(narrow_sent[layer])

    def returned(turn):
        return outer_sum(seat_matrix(turn), grad_embedded).astype(low).reshape(devices, slots_each, width)

    came = lax.all_to_all(returned(0), BOTH, 0, 0, tiled=True)

    def later_turn(carry):
        turn, total = carry
        rows = lax.all_to_all(returned(turn), BOTH, 0, 0, tiled=True).reshape(slots_all, width)
        return (turn + 1, total + outer_sum(wanted_of(requests(turn)), rows))

    _, table_grad = lax.while_loop(lambda carry: carry[0] < turns, later_turn, (jnp.int32(1), table_grad))
    table_sum = table_grad + outer_sum(wanted_of(heard_first), came.reshape(slots_all, width))
    for layer in range(1, layers):
        narrow_sent[layer] = send_deep(narrow_sent[layer])
    wide_sent[0] = send_deep(wide_sent[0])
    narrow_sent[0] = send_deep(narrow_sent[0])
    wide_sums = [sum_low(sent) for sent in wide_sent]
    narrow_sums = [sum_low(sent) for sent in narrow_sent]

    contract_sum = jnp.stack([total[:hidden_share] for total in wide_sums])
    expand_sum = jnp.stack(
        [rows_to_lanes(total[hidden_share:], hidden_width // width) for total in wide_sums]
    )
    attend_sum = jnp.stack([rows_to_lanes(total[: 3 * row_share], 3) for total in narrow_sums])
    project_sum = jnp.stack([total[3 * row_share : 4 * row_share] for total in narrow_sums])
    small_sum = narrow_sums[0][4 * row_share :]
    position_sum = small_sum[:position_share]
    vector_sum = small_sum[position_share : position_share + vector_rows].reshape(-1)[:vector_share]

    sums = (table_sum, position_sum, attend_sum, project_sum, expand_sum, contract_sum, vector_sum)
    squares = jnp.zeros((), jnp.float32)
    for grad in sums:
        squares = squares + jnp.sum(grad * grad)
    scalars = jnp.stack([squares, entropy_local, jnp.sum(loss_mask).astype(jnp.float32)])
    square_total, entropy_total, count = jnp.sum(spread(scalars).reshape(devices, 3), axis=0)
    grad_norm = jnp.sqrt(square_total) / count
    factor = clip_limit / jnp.maximum(grad_norm, clip_limit)
    loss = entropy_total / count
    weights = (
        token_table,
        position_table,
        attend_weight,
        project_weight,
        expand_weight,
        contract_weight,
        vector_params,
    )
    moments = (
        table_moments,
        position_moments,
        attend_moments,
        project_moments,
        expand_moments,
        contract_moments,
        vector_moments,
    )
    decays = (decay_rate, decay_rate, decay_rate, decay_rate, decay_rate, decay_rate, 0.0)

    def updated(weight, moment, grad, decay):
        if weight.ndim < 2:
            return adam_update(weight, moment, grad / count * factor, decay)
        lanes = weight.shape[-1]
        fresh, pair, copy = adam_blocks(
            weight.reshape(-1, lanes), moment.reshape(2, -1, lanes), grad.reshape(-1, lanes), count, factor, decay
        )
        return (fresh.reshape(weight.shape), pair.reshape(moment.shape), copy.reshape(weight.shape))

    table_new, position_new, attend_new, project_new, expand_new, contract_new, vector_new = [
        updated(weight, moment, grad, decay)
        for weight, moment, grad, decay in zip(weights, moments, sums, decays)
    ]
    return (
        loss,
        grad_norm,
        table_new[0],
        position_new[0],
        attend_new[0],
        project_new[0],
        expand_new[0],
        contract_new[0],
        vector_new[0],
        table_new[1],
        position_new[1],
        attend_new[1],
        project_new[1],
        expand_new[1],
        contract_new[1],
        vector_new[1],
        table_new[2],
        position_new[2],
        attend_new[2],
        project_new[2],
        expand_new[2],
        contract_new[2],
        vector_new[2],
    )


def solution(mesh):
    return jax.shard_map(
        shards,
        mesh=mesh,
        in_specs=(
            P(None, ("dp", "fsdp"), None),
            P(None, ("dp", "fsdp"), None),
            P(None, ("dp", "fsdp"), None),
            P(None, ("dp", "fsdp"), None),
            P(None, ("dp", "fsdp"), None),
            P(None, ("dp", "fsdp"), None),
            P(("dp", "fsdp"), None),
            P(("dp", "fsdp"), None),
            P(None, ("dp", "fsdp"), None),
            P(None, ("dp", "fsdp"), None),
            P(None, ("dp", "fsdp"), None),
            P(None, ("dp", "fsdp"), None),
            P(("dp", "fsdp")),
            P(None, ("dp", "fsdp"), None),
            P(None, ("dp", "fsdp"), None),
            P(None, None, ("dp", "fsdp"), None),
            P(None, None, ("dp", "fsdp"), None),
            P(None, None, ("dp", "fsdp"), None),
            P(None, None, ("dp", "fsdp"), None),
            P(None, ("dp", "fsdp")),
        ),
        out_specs=(
            P(),
            P(),
            P(("dp", "fsdp"), None),
            P(("dp", "fsdp"), None),
            P(None, ("dp", "fsdp"), None),
            P(None, ("dp", "fsdp"), None),
            P(None, ("dp", "fsdp"), None),
            P(None, ("dp", "fsdp"), None),
            P(("dp", "fsdp")),
            P(None, ("dp", "fsdp"), None),
            P(None, ("dp", "fsdp"), None),
            P(None, None, ("dp", "fsdp"), None),
            P(None, None, ("dp", "fsdp"), None),
            P(None, None, ("dp", "fsdp"), None),
            P(None, None, ("dp", "fsdp"), None),
            P(None, ("dp", "fsdp")),
            P(("dp", "fsdp"), None),
            P(("dp", "fsdp"), None),
            P(None, ("dp", "fsdp"), None),
            P(None, ("dp", "fsdp"), None),
            P(None, ("dp", "fsdp"), None),
            P(None, ("dp", "fsdp"), None),
            P(("dp", "fsdp")),
        ),
        check_vma=False,
    )
```
